512 devices in a mesh: gx: 8 (over y), gy: 8 (over x, z_lo), gz: 8 (over z_hi, core).
Axes of the slice: x: 4, y: 8, z: 8 (z_hi: 4, z_lo: 2; z = z_hi * 2 + z_lo), core: 2. Of those that a mesh axis runs over, the one named last changes fastest.
Arguments:
- features: bfloat16 [64, 32, 32, 512], P('gx', 'gy', 'gz'), may hold values from -31 to 31, as said below
- grad_y: bfloat16 [64, 32, 32, 512], P('gx', 'gy', 'gz'), may hold values from -6 to 6
- attn_out: bfloat16 [64, 32, 32, 512], P('gx', 'gy', 'gz'), may hold values from -3 to 3
- w_query: bfloat16 [512, 512], P('gz'), may hold values from -0.25 to 0.25
- w_key: bfloat16 [512, 512], P('gz'), may hold values from -0.25 to 0.25
- w_value: bfloat16 [512, 512], P('gz'), may hold values from -0.25 to 0.25
- w_out: bfloat16 [512, 512], P('gz'), may hold values from -0.25 to 0.25
Outputs:
- grad_x: bfloat16 [64, 32, 32, 512], P('gx', 'gy', 'gz')
- grad_query: float32 [512, 512], P('gz')
- grad_key: float32 [512, 512], P('gz')
- grad_value: float32 [512, 512], P('gz')
- grad_out: float32 [512, 512], P('gz')
The draws below stay inside these ranges and needn't reach their ends.
Inputs may be any that keep to these rules, and one draw needn't show every extreme that they name: features of the patch tokens.
All inputs are finite; a program needn't handle non-finite values.
Results may differ from the reference program's by a relative error of at most 0.018.
Values may be sent and summed in bfloat16 or wider, within the bound.
A program may use at most 64 MiB of HBM per device.

```python
import math
import jax
import jax.numpy as jnp
from jax import lax

D = 512
HEADS = 8
B = 8
NX = 64
NY = 32
NZ = 32


def draw_features(key, part):
    first, second = jax.random.split(key, 2)
    field_shape = (NX, NY, NZ, D)
    token_scale = jnp.exp(jax.random.uniform(second, (NX, NY, NZ, 1), jnp.float32, math.log(0.3), math.log(3.0)))
    values = jax.random.truncated_normal(first, -4.0, 4.0, field_shape, jnp.float32) * token_scale
    return values.astype(jnp.bfloat16)


def levels(key, shape, cuts, least, largest):
    loudness = 1.0
    for axis_at, shards_of in cuts:
        draws = jax.random.uniform(jax.random.fold_in(jax.random.fold_in(key, 6), axis_at), (shards_of,), jnp.float32, least / len(cuts), largest / len(cuts))
        loudness = loudness * jnp.repeat(jnp.exp(draws), shape[axis_at] // shards_of).reshape((-1,) + (1,) * (len(shape) - 1 - axis_at))
    return loudness


def noise(stream_key, extent, scale, limit, shards=(), held_as=jnp.bfloat16):
    result = jax.random.normal(stream_key, extent, jnp.float32) * scale
    if len(shards) > 0:
        result = levels(stream_key, extent, shards, -0.22, 0.18) * result
    return jnp.clip(result, min=-limit, max=limit).astype(held_as)


def setup_inputs(seed: int = 0) -> dict:
    key_of = jax.random.split(jax.random.key(seed), 8)
    features = draw_features(jax.random.fold_in(key_of[7], 71), 0)
    grad_y = noise(key_of[1], (NX, NY, NZ, D), 1.0, 6.0, ((0, 8), (1, 8), (2, 8)))
    attn_out = noise(key_of[2], (NX, NY, NZ, D), 0.5, 3.0, ((0, 8), (1, 8), (2, 8)))
    w_query = noise(key_of[3], (D, D), D ** -0.5, 0.25, ((0, 8),))
    w_key = noise(key_of[4], (D, D), D ** -0.5, 0.25, ((0, 8),))
    w_value = noise(key_of[5], (D, D), D ** -0.5, 0.25, ((0, 8),))
    w_out = noise(key_of[6], (D, D), D ** -0.5, 0.25, ((0, 8),))
    return dict(features=features, grad_y=grad_y, attn_out=attn_out, w_query=w_query, w_key=w_key, w_value=w_value, w_out=w_out)


NEIGHBOURS = ((0, 0, 0), (-1, 0, 0), (1, 0, 0), (0, -1, 0), (0, 1, 0), (0, 0, -1), (0, 0, 1))

def to_blocks(field, block_edge):
    count_x = field.shape[0] // block_edge
    count_y = field.shape[1] // block_edge
    count_z = field.shape[2] // block_edge
    width = field.shape[3]
    split_field = field.reshape(count_x, block_edge, count_y, block_edge, count_z, block_edge, width)
    return split_field.transpose(0, 2, 4, 1, 3, 5, 6).reshape(count_x, count_y, count_z, block_edge ** 3, width)

def from_blocks(blocks, block_edge):
    count_x, count_y, count_z, unused, width = blocks.shape
    split_field = blocks.reshape(count_x, count_y, count_z, block_edge, block_edge, block_edge, width)
    return split_field.transpose(0, 3, 1, 4, 2, 5, 6).reshape(count_x * block_edge, count_y * block_edge, count_z * block_edge, width)

def reference(features, grad_y, attn_out, w_query, w_key, w_value, w_out):
    field_shape = features.shape
    width = field_shape[3]
    head_dim = width // HEADS
    score_scale = 1.0 / math.sqrt(head_dim)
    block_tokens = B ** 3
    feature_rows = features.reshape(-1, width)
    dy_rows = grad_y.reshape(-1, width)
    saved_rows = attn_out.reshape(-1, width)
    query = jnp.dot(feature_rows, w_query, preferred_element_type=jnp.float32).astype(jnp.bfloat16)
    key_rows = jnp.dot(feature_rows, w_key, preferred_element_type=jnp.float32).astype(jnp.bfloat16)
    value_rows = jnp.dot(feature_rows, w_value, preferred_element_type=jnp.float32).astype(jnp.bfloat16)
    out_grad = jnp.dot(dy_rows, w_out.T, preferred_element_type=jnp.float32).astype(jnp.bfloat16)
    query_blocks = to_blocks(query.reshape(field_shape), B)
    key_blocks = to_blocks(key_rows.reshape(field_shape), B)
    value_blocks = to_blocks(value_rows.reshape(field_shape), B)
    grad_blocks = to_blocks(out_grad.reshape(field_shape), B)
    saved_blocks = to_blocks(attn_out, B)
    count_x, count_y, count_z = query_blocks.shape[:3]

    def block_step(carry, index):
        key_total, value_total = carry
        place_x = index // (count_y * count_z)
        place_y = index // count_z % count_y
        place_z = index % count_z
        spots = []
        for step_x, step_y, step_z in NEIGHBOURS:
            spots.append(((place_x + step_x) % count_x, (place_y + step_y) % count_y, (place_z + step_z) % count_z))
        near_keys = jnp.concatenate([key_blocks[spot] for spot in spots])
        near_values = jnp.concatenate([value_blocks[spot] for spot in spots])
        key_heads = near_keys.astype(jnp.float32).reshape(7 * block_tokens, HEADS, head_dim)
        value_heads = near_values.astype(jnp.float32).reshape(7 * block_tokens, HEADS, head_dim)
        query_heads = query_blocks[place_x, place_y, place_z].astype(jnp.float32).reshape(block_tokens, HEADS, head_dim)
        grad_heads = grad_blocks[place_x, place_y, place_z].astype(jnp.float32).reshape(block_tokens, HEADS, head_dim)
        saved_heads = saved_blocks[place_x, place_y, place_z].astype(jnp.float32).reshape(block_tokens, HEADS, head_dim)
        scores = jnp.einsum('qhd,khd->hqk', query_heads, key_heads) * score_scale
        row_top = lax.optimization_barrier(jnp.max(scores, axis=2, keepdims=True))
        log_total = row_top + jnp.log(lax.optimization_barrier(jnp.sum(jnp.exp(scores - row_top), axis=2, keepdims=True)))
        attn_prob = jnp.exp(scores - log_total).astype(jnp.bfloat16)
        prob_grad = jnp.einsum('qhd,khd->hqk', grad_heads, value_heads)
        row_delta = lax.optimization_barrier(jnp.sum(grad_heads * saved_heads, axis=2)).T[:, :, None]
        score_grad = (attn_prob.astype(jnp.float32) * (prob_grad - row_delta) * score_scale).astype(jnp.bfloat16)
        query_grad = jnp.einsum('hqk,khd->qhd', score_grad.astype(jnp.float32), key_heads).reshape(block_tokens, width).astype(jnp.bfloat16)
        key_part = jnp.einsum('hqk,qhd->khd', score_grad.astype(jnp.float32), query_heads).astype(jnp.bfloat16).reshape(7, block_tokens, width)
        value_part = jnp.einsum('hqk,qhd->khd', attn_prob.astype(jnp.float32), grad_heads).astype(jnp.bfloat16).reshape(7, block_tokens, width)
        for slot_index in range(7):
            spot = spots[slot_index]
            key_total = key_total.at[spot].add(key_part[slot_index].astype(jnp.float32))
            value_total = value_total.at[spot].add(value_part[slot_index].astype(jnp.float32))
        return ((key_total, value_total), query_grad)
    zero_blocks = jnp.zeros(query_blocks.shape, jnp.float32)
    block_count = count_x * count_y * count_z
    totals, query_grads = lax.scan(block_step, (zero_blocks, zero_blocks), jnp.arange(block_count, dtype=jnp.int32))
    query_act_grad = from_blocks(query_grads.reshape(query_blocks.shape), B).reshape(-1, width)
    key_act_grad = from_blocks(totals[0].astype(jnp.bfloat16), B).reshape(-1, width)
    value_act_grad = from_blocks(totals[1].astype(jnp.bfloat16), B).reshape(-1, width)
    grad_x = jnp.dot(query_act_grad, w_query.T, preferred_element_type=jnp.float32)
    grad_x = grad_x + jnp.dot(key_act_grad, w_key.T, preferred_element_type=jnp.float32)
    grad_x = grad_x + jnp.dot(value_act_grad, w_value.T, preferred_element_type=jnp.float32)
    grad_x = grad_x.astype(jnp.bfloat16).reshape(field_shape)
    grad_query = jnp.dot(feature_rows.T, query_act_grad, preferred_element_type=jnp.float32)
    grad_key = jnp.dot(feature_rows.T, key_act_grad, preferred_element_type=jnp.float32)
    grad_value = jnp.dot(feature_rows.T, value_act_grad, preferred_element_type=jnp.float32)
    grad_out = jnp.dot(saved_rows.T, dy_rows, preferred_element_type=jnp.float32)
    return (grad_x, grad_query, grad_key, grad_value, grad_out)
```

```python
import functools
import math

import jax
import jax.numpy as jnp
from jax import lax
from jax.experimental import pallas as pl
from jax.experimental.pallas import tpu as pltpu
from jax.sharding import PartitionSpec as P

HEADS = 8
MESH = pl.DeviceIdType.MESH
STEPS = (("gx", 1), ("gx", -1), ("gy", 2), ("gy", -2), ("gz", 2), ("gz", -2))
BF16 = jnp.bfloat16
F32 = jnp.float32


def remote(src, dst, send, recv, device):
    return pltpu.make_async_remote_copy(
        src_ref=src, dst_ref=dst, send_sem=send, recv_sem=recv, device_id=device, device_id_type=MESH
    )


def greet(devices):
    barrier = pltpu.get_barrier_semaphore()
    for device in devices:
        pl.semaphore_signal(barrier, inc=1, device_id=device, device_id_type=MESH)
    pl.semaphore_wait(barrier, len(devices))


def ring(axis, index, step):
    return {axis: lax.rem(index + step + 8, 8)}


def gather_kernel(
    f_ref, g_ref, a_ref, wq_ref, wk_ref, wv_ref, wo_ref,
    fb_ref, gb_ref, ab_ref, w3_ref, wob_ref,
    bsend, brecv, wsend, wrecv, osend, orecv,
):
    gy, gz = lax.axis_index("gy"), lax.axis_index("gz")
    y_bit, z_bit = lax.rem(gy, 2), lax.rem(gz, 2)
    pair_z = {"gz": gz + 1 - 2 * z_bit}
    pair_y = {"gy": gy + 1 - 2 * y_bit}
    slot = 2 * y_bit + z_bit
    slot_y = 2 * (1 - y_bit) + z_bit
    greet([ring("gz", gz, d) for d in range(1, 8)] + [pair_y])
    trios = ((f_ref, fb_ref), (g_ref, gb_ref), (a_ref, ab_ref))
    to_y, to_z, onward = [], [], []
    for i, (src, dst) in enumerate(trios):
        to_y.append(remote(src, dst.at[slot], bsend.at[0, i], brecv.at[0, i], pair_y))
        to_z.append(remote(src, dst.at[slot], bsend.at[1, i], brecv.at[1, i], pair_z))
        to_y[-1].start()
        to_z[-1].start()
    weights = (wq_ref, wk_ref, wv_ref)
    rows = pl.ds(pl.multiple_of(gz * 64, 64), 64)
    weight_copies = []
    for d in (4, 3, 5, 2, 6, 1, 7):
        target = lax.rem(gz + d, 8)
        columns = pl.ds(pl.multiple_of(lax.rem(target, 2) * 256 + y_bit * 128, 128), 128)
        for i, w_ref in enumerate(weights):
            copy = remote(
                w_ref.at[:, columns], w3_ref.at[i, rows], wsend.at[d - 1, i], wrecv.at[d - 1, i], {"gz": target}
            )
            copy.start()
            weight_copies.append(copy)
    half = lax.rem(gz, 2)
    out_core = lax.div(gz, 4)
    out_from = lax.rem(lax.div(gz, 2), 2) == y_bit
    out_rows = pl.ds(pl.multiple_of(half * 64, 64), 64)

    def out_copy(zh):
        return remote(wo_ref, wob_ref.at[out_rows], osend.at[zh], orecv.at[half], {"gz": 2 * zh + out_core})

    for zh in range(4):

        @pl.when(jnp.logical_and(out_from, 2 * zh + out_core != gz))
        def _():
            out_copy(zh).start()

    columns = pl.ds(pl.multiple_of(z_bit * 256 + y_bit * 128, 128), 128)
    for i, w_ref in enumerate(weights):
        w3_ref[i, rows] = w_ref[:, columns]
    for src, dst in trios:
        dst[slot] = src[...]
    for i, (src, dst) in enumerate(trios):
        to_y[i].wait_recv()
        onward.append(remote(dst.at[slot_y], dst.at[slot_y], bsend.at[2, i], brecv.at[2, i], pair_z))
        onward[-1].start()
    for s in range(2):
        source = 4 * z_bit + 2 * y_bit + s

        @pl.when(source != gz)
        def _():
            remote(wo_ref, wob_ref.at[pl.ds(s * 64, 64)], osend.at[0], orecv.at[s], {"gz": source}).wait_recv()

        @pl.when(source == gz)
        def _():
            wob_ref[pl.ds(s * 64, 64)] = wo_ref[...]

    for copy in weight_copies:
        copy.wait()
    for zh in range(4):

        @pl.when(jnp.logical_and(out_from, 2 * zh + out_core != gz))
        def _():
            out_copy(zh).wait_send()

    for i in range(3):
        to_y[i].wait_send()
        to_z[i].wait()
        onward[i].wait()


def swap_kernel(sign, src_ref, dst_ref, send, recv):
    index = {axis: lax.axis_index(axis) for axis in ("gx", "gy", "gz")}
    greet([ring(axis, index[axis], step) for axis, step in STEPS])
    copies = []
    for k in (4, 5, 0, 1, 2, 3):
        axis, step = STEPS[k]
        src = src_ref.at[k] if sign < 0 else src_ref
        copies.append(remote(src, dst_ref.at[k], send.at[k], recv.at[k], ring(axis, index[axis], sign * step)))
        copies[-1].start()
    for copy in copies:
        copy.wait()


def reduce_kernel(
    t_ref, g_ref, h_ref, gx_ref,
    xr, s1, yr, s2, zr, u, gr,
    xsend, xrecv, ysend, yrecv, zsend, zrecv, usend, urecv, hsend, hrecv, gsend, grecv,
):
    gx, gy, gz = (lax.axis_index(axis) for axis in ("gx", "gy", "gz"))
    y_bit, z_bit = lax.rem(gy, 2), lax.rem(gz, 2)
    x = lax.div(gy, 2)
    other_z, other_y = gz + 1 - 2 * z_bit, gy + 1 - 2 * y_bit
    greet(
        [ring("gy", gy, d) for d in range(1, 8)]
        + [ring("gx", gx, d) for d in range(1, 8)]
        + [ring("gz", gz, d) for d in range(1, 8)]
        + [{"gy": other_y, "gz": other_z}]
    )

    def run(copies):
        for copy in copies:
            copy.start()
        return copies

    def join(copies):
        for copy in copies:
            copy.wait()

    x_copies = []
    for d in (2, 1, 3):
        target = lax.rem(x + d, 4)
        x_copies.append(
            remote(t_ref.at[target], xr.at[d - 1], xsend.at[d - 1], xrecv.at[d - 1], {"gy": 2 * target + y_bit})
        )
    run(x_copies)
    parts = (
        (2 * (1 - y_bit) + 1 - z_bit, {"gy": other_y, "gz": other_z}),
        (2 * (1 - y_bit) + z_bit, {"gy": other_y}),
        (2 * y_bit + 1 - z_bit, {"gz": other_z}),
    )
    g_copies = run(
        [remote(g_ref.at[part], gr.at[k], gsend.at[k], grecv.at[k], dev) for k, (part, dev) in enumerate(parts)]
    )
    join(x_copies)
    total = t_ref[x].astype(F32)
    for d in range(3):
        total = total + xr[d].astype(F32)
    s1[...] = total.astype(BF16)
    y_copies = []
    for d in (4, 3, 5, 2, 6, 1, 7):
        target = lax.rem(gx + d, 8)
        y_copies.append(remote(s1.at[target], yr.at[d - 1], ysend.at[d - 1], yrecv.at[d - 1], {"gx": target}))
    run(y_copies)
    join(y_copies)
    total = s1[gx].astype(F32)
    for d in range(7):
        total = total + yr[d].astype(F32)
    s2[...] = total.reshape(8, 8, 128)
    z_copies = []
    for d in (4, 3, 5, 2, 6, 1, 7):
        target = lax.rem(gz + d, 8)
        z_copies.append(remote(s2.at[target], zr.at[gz], zsend.at[d - 1], zrecv.at[d - 1], {"gz": target}))
    run(z_copies)
    zr[gz] = s2[gz]
    join(z_copies)
    lower = zr[0] + zr[2] + zr[4] + zr[6]
    upper = zr[1] + zr[3] + zr[5] + zr[7]
    u[gx] = jnp.concatenate([lower, upper], axis=0).astype(BF16)
    u_copies = []
    for d in (4, 3, 5, 2, 6, 1, 7):
        u_copies.append(remote(u.at[gx], u.at[gx], usend.at[d - 1], urecv.at[d - 1], ring("gx", gx, d)))
    run(u_copies)
    join(g_copies)
    total = g_ref[2 * y_bit + z_bit].astype(F32)
    for k in range(3):
        total = total + gr[k].astype(F32)
    gx_ref[...] = total.astype(BF16)
    join(u_copies)
    h_copies = []
    for d in (4, 3, 5, 2, 6, 1, 7):
        h_copies.append(remote(u, h_ref.at[gy], hsend.at[d - 1], hrecv.at[d - 1], ring("gy", gy, d)))
    run(h_copies)
    h_ref[gy] = u[...]
    join(h_copies)


def vmem(count):
    return [pl.BlockSpec(memory_space=pltpu.VMEM)] * count


def dma(*shape):
    return pltpu.SemaphoreType.DMA(shape)


def call(kernel, number, shapes, scratch, *operands):
    return pl.pallas_call(
        kernel,
        out_shape=[jax.ShapeDtypeStruct(shape, BF16) for shape in shapes],
        in_specs=vmem(len(operands)),
        out_specs=vmem(len(shapes)),
        scratch_shapes=scratch,
        compiler_params=pltpu.CompilerParams(collective_id=number, has_side_effects=True),
    )(*operands)


def transpose_dot(left, right):
    return lax.dot_general(left, right, (((1,), (1,)), ((), ())), preferred_element_type=F32)


def token_dot(left, right):
    return lax.dot_general(left, right, (((0,), (0,)), ((), ())), preferred_element_type=F32)


def dot(left, right):
    return jnp.dot(left, right, preferred_element_type=F32)


def attention(query, grad, row_delta, nearby):
    tokens, quarter = query.shape
    head_dim = 64
    group_heads = quarter // head_dim
    score_scale = 1.0 / math.sqrt(head_dim)
    query_heads = query.reshape(tokens, group_heads, head_dim)
    grad_heads = grad.reshape(tokens, group_heads, head_dim)

    def first_pass(carry, key_value):
        row_top, row_total = carry
        key_heads = key_value[0].reshape(tokens, group_heads, head_dim)
        scores = jnp.einsum("qhd,khd->hqk", query_heads, key_heads, preferred_element_type=F32) * score_scale
        new_top = jnp.maximum(row_top, jnp.max(scores, axis=2))
        row_total = row_total * jnp.exp(row_top - new_top) + jnp.sum(jnp.exp(scores - new_top[:, :, None]), axis=2)
        return ((new_top, row_total), None)

    start_top = jnp.full((group_heads, tokens), -jnp.inf, F32)
    start_total = jnp.zeros((group_heads, tokens), F32)
    stats, unused = lax.scan(first_pass, (start_top, start_total), nearby)
    log_total = stats[0] + jnp.log(stats[1])

    def second_pass(query_grad, key_value):
        key_heads = key_value[0].reshape(tokens, group_heads, head_dim)
        value_heads = key_value[1].reshape(tokens, group_heads, head_dim)
        scores = jnp.einsum("qhd,khd->hqk", query_heads, key_heads, preferred_element_type=F32) * score_scale
        prob = jnp.exp(scores - log_total[:, :, None]).astype(BF16)
        prob_grad = jnp.einsum("qhd,khd->hqk", grad_heads, value_heads, preferred_element_type=F32)
        score_grad = (prob.astype(F32) * (prob_grad - row_delta[:, :, None]) * score_scale).astype(BF16)
        query_grad = query_grad + jnp.einsum("hqk,khd->qhd", score_grad, key_heads, preferred_element_type=F32)
        key_grad = jnp.einsum("hqk,qhd->khd", score_grad, query_heads, preferred_element_type=F32)
        value_grad = jnp.einsum("hqk,qhd->khd", prob, grad_heads, preferred_element_type=F32)
        key_grad = key_grad.astype(BF16).reshape(tokens, quarter)
        value_grad = value_grad.astype(BF16).reshape(tokens, quarter)
        return (query_grad, jnp.stack([key_grad, value_grad]))

    start_grad = jnp.zeros((tokens, group_heads, head_dim), F32)
    query_grad, partials = lax.scan(second_pass, start_grad, nearby)
    return query_grad.reshape(tokens, quarter).astype(BF16), partials


def on_device(features, grad_y, attn_out, w_query, w_key, w_value, w_out):
    width = features.shape[3]
    local = features.shape[0] * features.shape[1] * features.shape[2]
    tokens = 4 * local
    quarter = width // 4
    feature_rows = features.reshape(local, width)
    dy_rows = grad_y.reshape(local, width)
    saved_rows = attn_out.reshape(local, width)
    fb, gb, ab, w3, wo = call(
        gather_kernel,
        0,
        [(4, local, width)] * 3 + [(3, width, quarter), (quarter, width)],
        [dma(3, 3), dma(3, 3), dma(7, 3), dma(7, 3), dma(4), dma(2)],
        feature_rows, dy_rows, saved_rows, w_query, w_key, w_value, w_out,
    )
    fb, gb, ab = (block.reshape(tokens, width) for block in (fb, gb, ab))
    start = (lax.axis_index("gz") % 2) * (2 * quarter) + (lax.axis_index("gy") % 2) * quarter
    own_gb = lax.dynamic_slice_in_dim(gb, start, quarter, 1)
    own_ab = lax.dynamic_slice_in_dim(ab, start, quarter, 1)
    query, key, value = (dot(fb, w3[i]).astype(BF16) for i in range(3))
    grad = transpose_dot(gb, wo).astype(BF16)
    own_pair = jnp.stack([key, value])
    (near,) = call(
        functools.partial(swap_kernel, 1), 1, [(6, 2, tokens, quarter)], [dma(6), dma(6)], own_pair
    )
    products = grad.astype(F32) * own_ab.astype(F32)
    row_delta = jnp.sum(products.reshape(tokens, 2, quarter // 2), axis=2).T
    query_grad, partials = attention(query, grad, row_delta, jnp.concatenate([own_pair[None], near]))
    (back,) = call(
        functools.partial(swap_kernel, -1), 2, [(6, 2, tokens, quarter)], [dma(6), dma(6)], partials[1:]
    )
    pair_grads = (partials[0].astype(F32) + jnp.sum(back.astype(F32), axis=0)).astype(BF16)
    grads = (query_grad, pair_grads[0], pair_grads[1])
    partial_x = sum(transpose_dot(grads[i], w3[i]) for i in range(3))
    partial_x = partial_x.astype(BF16).reshape(4, local, width)
    terms = jnp.stack([token_dot(fb, part) for part in grads] + [token_dot(ab, own_gb)])
    terms = terms.astype(BF16).reshape(4, 8, 8, 8, quarter).transpose(0, 2, 1, 3, 4)
    terms = terms.reshape(4, 8, 64, quarter)
    rows, grad_x = call(
        reduce_kernel,
        3,
        [(8, 8, 16, quarter), (local, width)],
        [
            pltpu.VMEM((3, 8, 64, quarter), BF16),
            pltpu.VMEM((8, 64, quarter), BF16),
            pltpu.VMEM((7, 64, quarter), BF16),
            pltpu.VMEM((8, 8, quarter), F32),
            pltpu.VMEM((8, 8, quarter), F32),
            pltpu.VMEM((8, 16, quarter), BF16),
            pltpu.VMEM((3, local, width), BF16),
            dma(3), dma(3), dma(7), dma(7), dma(7), dma(7), dma(7), dma(7), dma(7), dma(7), dma(3), dma(3),
        ],
        terms, partial_x,
    )
    rows = rows.astype(F32).reshape(4, 2, 8, 2, 8, quarter).transpose(0, 2, 4, 3, 1, 5).reshape(4, 64, width)
    return (grad_x.reshape(features.shape), rows[0], rows[1], rows[2], rows[3])


def solution(mesh):
    token_spec = P("gx", "gy", "gz", None)
    row_spec = P("gz", None)
    return jax.shard_map(
        on_device,
        mesh=mesh,
        in_specs=(token_spec,) * 3 + (row_spec,) * 4,
        out_specs=(token_spec,) + (row_spec,) * 4,
        check_vma=False,
    )
```

```python
import jax
import jax.numpy as jnp
from jax import lax
from jax.experimental import pallas as pl
from jax.experimental.pallas import tpu as pltpu
from jax.sharding import PartitionSpec as P

HEADS = 8
MESH = pl.DeviceIdType.MESH
STEPS = (("gx", 1), ("gx", -1), ("gy", 2), ("gy", -2), ("gz", 2), ("gz", -2))
BF16 = jnp.bfloat16
F32 = jnp.float32


def remote(src, dst, send, recv, device):
    return pltpu.make_async_remote_copy(
        src_ref=src, dst_ref=dst, send_sem=send, recv_sem=recv, device_id=device, device_id_type=MESH
    )


def greet(devices):
    barrier = pltpu.get_barrier_semaphore()
    for device in devices:
        pl.semaphore_signal(barrier, inc=1, device_id=device, device_id_type=MESH)
    pl.semaphore_wait(barrier, len(devices))


def ring(axis, index, step):
    return {axis: lax.rem(index + step + 8, 8)}


def gather_kernel(
    f_ref, g_ref, a_ref, wq_ref, wk_ref, wv_ref, wo_ref,
    fb_ref, gb_ref, ab_ref, w3_ref, wob_ref,
    bsend, brecv, wsend, wrecv, osend, orecv,
):
    gy, gz = lax.axis_index("gy"), lax.axis_index("gz")
    y_bit, z_bit = lax.rem(gy, 2), lax.rem(gz, 2)
    pair_z = {"gz": gz + 1 - 2 * z_bit}
    pair_y = {"gy": gy + 1 - 2 * y_bit}
    slot = 2 * y_bit + z_bit
    slot_y = 2 * (1 - y_bit) + z_bit
    greet([ring("gz", gz, d) for d in range(1, 8)] + [pair_y])
    trios = ((f_ref, fb_ref), (g_ref, gb_ref), (a_ref, ab_ref))
    to_y, to_z, onward = [], [], []
    for i, (src, dst) in enumerate(trios):
        to_y.append(remote(src, dst.at[slot], bsend.at[0, i], brecv.at[0, i], pair_y))
        to_z.append(remote(src, dst.at[slot], bsend.at[1, i], brecv.at[1, i], pair_z))
        to_y[-1].start()
        to_z[-1].start()
    weights = (wq_ref, wk_ref, wv_ref)
    rows = pl.ds(pl.multiple_of(gz * 64, 64), 64)
    weight_copies = []
    for d in (4, 3, 5, 2, 6, 1, 7):
        target = lax.rem(gz + d, 8)
        columns = pl.ds(pl.multiple_of(lax.rem(target, 2) * 256 + y_bit * 128, 128), 128)
        for i, w_ref in enumerate(weights):
            copy = remote(
                w_ref.at[:, columns], w3_ref.at[i, rows], wsend.at[d - 1, i], wrecv.at[d - 1, i], {"gz": target}
            )
            copy.start()
            weight_copies.append(copy)
    half = lax.rem(gz, 2)
    out_core = lax.div(gz, 4)
    out_from = lax.rem(lax.div(gz, 2), 2) == y_bit
    out_rows = pl.ds(pl.multiple_of(half * 64, 64), 64)

    def out_copy(zh):
        return remote(wo_ref, wob_ref.at[out_rows], osend.at[zh], orecv.at[half], {"gz": 2 * zh + out_core})

    for zh in range(4):

        @pl.when(jnp.logical_and(out_from, 2 * zh + out_core != gz))
        def _():
            out_copy(zh).start()

    columns = pl.ds(pl.multiple_of(z_bit * 256 + y_bit * 128, 128), 128)
    for i, w_ref in enumerate(weights):
        w3_ref[i, rows] = w_ref[:, columns]
    for src, dst in trios:
        dst[slot] = src[...]
    for i, (src, dst) in enumerate(trios):
        to_y[i].wait_recv()
        onward.append(remote(dst.at[slot_y], dst.at[slot_y], bsend.at[2, i], brecv.at[2, i], pair_z))
        onward[-1].start()
    for s in range(2):
        source = 4 * z_bit + 2 * y_bit + s

        @pl.when(source != gz)
        def _():
            remote(wo_ref, wob_ref.at[pl.ds(s * 64, 64)], osend.at[0], orecv.at[s], {"gz": source}).wait_recv()

        @pl.when(source == gz)
        def _():
            wob_ref[pl.ds(s * 64, 64)] = wo_ref[...]

    for copy in weight_copies:
        copy.wait()
    for zh in range(4):

        @pl.when(jnp.logical_and(out_from, 2 * zh + out_core != gz))
        def _():
            out_copy(zh).wait_send()

    for i in range(3):
        to_y[i].wait_send()
        to_z[i].wait()
        onward[i].wait()


def attend_kernel(
    q_ref, g_ref, delta_ref, own_ref, dq_ref, dkv_ref,
    kv, scores, part, back, qt, gt, kt, qs, gs, prob, grad, dqt, top, total,
    ksend, krecv, bsend, brecv,
):
    index = {axis: lax.axis_index(axis) for axis in ("gx", "gy", "gz")}
    tokens, width = q_ref.shape
    chunk = tokens // 2
    greet([ring(axis, index[axis], step) for axis, step in STEPS])

    def outward(i, k):
        axis, step = STEPS[k]
        return remote(own_ref.at[i], kv.at[k + 1, i], ksend.at[i, k + 1], krecv.at[i, k + 1], ring(axis, index[axis], step))

    def homeward(slot):
        pair = lax.div(slot - 1, 2)
        sign = 1 - 2 * lax.rem(slot - 1, 2)
        at_z = lax.div(pair, 2)
        at_y = pair - 2 * at_z
        at_x = 1 - at_y - at_z
        device = {
            "gx": lax.rem(index["gx"] - at_x * sign + 8, 8),
            "gy": lax.rem(index["gy"] - 2 * at_y * sign + 8, 8),
            "gz": lax.rem(index["gz"] - 2 * at_z * sign + 8, 8),
        }
        return remote(part.at[slot], back.at[slot], bsend.at[slot], brecv.at[slot], device)

    for i in range(2):
        for k in (4, 5, 0, 1, 2, 3):
            outward(i, k).start()

    kv[0] = own_ref[...]
    scaled = q_ref[...].astype(F32) * 0.125
    upstream = g_ref[...].astype(F32)
    row_head = lax.broadcasted_iota(jnp.int32, (width, tokens), 0) // (width // 2)
    lane_head = lax.broadcasted_iota(jnp.int32, (tokens, width), 1) // (width // 2)
    for value, turned, stacked in ((scaled, qt, qs), (upstream, gt, gs)):
        flipped = value.T
        for head in range(2):
            turned[:, head * tokens : (head + 1) * tokens] = jnp.where(row_head == head, flipped, 0.0).astype(BF16)
            stacked[head * tokens : (head + 1) * tokens, :] = jnp.where(lane_head == head, value, 0.0).astype(BF16)
    top[...] = jnp.full_like(top, -jnp.inf)
    total[...] = jnp.zeros_like(total)
    dqt[...] = jnp.zeros_like(dqt)

    def arrived(i, slot):
        return remote(own_ref.at[i], kv.at[slot, i], ksend.at[i, slot], krecv.at[i, slot], ring("gx", index["gx"], 1))

    def first_pass(slot, unused):
        @pl.when(slot > 0)
        def _():
            arrived(0, slot).wait_recv()

        for c in range(4):
            columns = slice(c * chunk, (c + 1) * chunk)
            block = dot(kv[slot, 0], qt[:, columns])
            scores[slot, :, columns] = block
            old_top = top[:, columns]
            new_top = jnp.maximum(old_top, jnp.max(block, axis=0, keepdims=True))
            summed = jnp.sum(jnp.exp(block - new_top), axis=0, keepdims=True)
            total[:, columns] = total[:, columns] * jnp.exp(old_top - new_top) + summed
            top[:, columns] = new_top
        return unused

    lax.fori_loop(0, 7, first_pass, 0)
    top[...] = top[...] + jnp.log(total[...])

    def second_pass(turn, unused):
        last = lax.div(turn, 6)
        group = lax.div(turn, 2)
        slot = (1 + 2 * (2 * group - 3 * lax.div(group, 2)) + lax.rem(turn, 2)) * (1 - last)

        @pl.when(turn < 6)
        def _():
            arrived(1, slot).wait_recv()

        kt[...] = kv[slot, 0].astype(F32).T.astype(BF16)
        for c in range(4):
            columns = slice(c * chunk, (c + 1) * chunk)
            p = jnp.exp(scores[slot, :, columns] - top[:, columns]).astype(BF16)
            prob[:, columns] = p
            dp = dot(kv[slot, 1], gt[:, columns])
            ds = (p.astype(F32) * (dp - delta_ref[:, columns])).astype(BF16)
            grad[:, columns] = ds
            dqt[:, columns] += dot(kt[...], ds)
        part[slot, 0] = dot(grad[...], qs[...]).astype(BF16)
        part[slot, 1] = dot(prob[...], gs[...]).astype(BF16)

        @pl.when(turn < 6)
        def _():
            homeward(slot).start()

        return unused

    lax.fori_loop(0, 7, second_pass, 0)
    half = width // 2
    turned = jnp.concatenate([dqt[:half, :tokens], dqt[half:, tokens:]], axis=0) * 0.125
    dq_ref[...] = turned.T.astype(BF16)
    for i in range(2):
        for k in range(6):
            outward(i, k).wait_send()
    for slot in (1, 2, 5, 6, 3, 4):
        homeward(slot).wait()
    for i in range(2):
        whole = part[0, i].astype(F32)
        for slot in range(1, 7):
            whole = whole + back[slot, i].astype(F32)
        dkv_ref[i] = whole.astype(BF16)


def reduce_kernel(
    t_ref, g_ref, h_ref, gx_ref,
    xr, s1, yr, s2, zr, u, gr,
    xsend, xrecv, ysend, yrecv, zsend, zrecv, usend, urecv, hsend, hrecv, gsend, grecv,
):
    gx, gy, gz = (lax.axis_index(axis) for axis in ("gx", "gy", "gz"))
    y_bit, z_bit = lax.rem(gy, 2), lax.rem(gz, 2)
    x = lax.div(gy, 2)
    other_z, other_y = gz + 1 - 2 * z_bit, gy + 1 - 2 * y_bit
    greet(
        [ring("gy", gy, d) for d in range(1, 8)]
        + [ring("gx", gx, d) for d in range(1, 8)]
        + [ring("gz", gz, d) for d in range(1, 8)]
        + [{"gy": other_y, "gz": other_z}]
    )

    def run(copies):
        for copy in copies:
            copy.start()
        return copies

    def join(copies):
        for copy in copies:
            copy.wait()

    x_copies = []
    for d in (2, 1, 3):
        target = lax.rem(x + d, 4)
        x_copies.append(
            remote(t_ref.at[target], xr.at[d - 1], xsend.at[d - 1], xrecv.at[d - 1], {"gy": 2 * target + y_bit})
        )
    run(x_copies)
    parts = (
        (2 * (1 - y_bit) + 1 - z_bit, {"gy": other_y, "gz": other_z}),
        (2 * (1 - y_bit) + z_bit, {"gy": other_y}),
        (2 * y_bit + 1 - z_bit, {"gz": other_z}),
    )
    g_copies = run(
        [remote(g_ref.at[part], gr.at[k], gsend.at[k], grecv.at[k], dev) for k, (part, dev) in enumerate(parts)]
    )
    join(x_copies)
    total = t_ref[x].astype(F32)
    for d in range(3):
        total = total + xr[d].astype(F32)
    s1[...] = total.astype(BF16)
    y_copies = []
    for d in (4, 3, 5, 2, 6, 1, 7):
        target = lax.rem(gx + d, 8)
        y_copies.append(remote(s1.at[target], yr.at[d - 1], ysend.at[d - 1], yrecv.at[d - 1], {"gx": target}))
    run(y_copies)
    join(y_copies)
    total = s1[gx].astype(F32)
    for d in range(7):
        total = total + yr[d].astype(F32)
    s2[...] = total.reshape(8, 8, 128)
    z_copies = []
    for d in (4, 3, 5, 2, 6, 1, 7):
        target = lax.rem(gz + d, 8)
        z_copies.append(remote(s2.at[target], zr.at[gz], zsend.at[d - 1], zrecv.at[d - 1], {"gz": target}))
    run(z_copies)
    zr[gz] = s2[gz]
    join(z_copies)
    lower = zr[0] + zr[2] + zr[4] + zr[6]
    upper = zr[1] + zr[3] + zr[5] + zr[7]
    u[gx] = jnp.concatenate([lower, upper], axis=0).astype(BF16)
    u_copies = []
    for d in (4, 3, 5, 2, 6, 1, 7):
        u_copies.append(remote(u.at[gx], u.at[gx], usend.at[d - 1], urecv.at[d - 1], ring("gx", gx, d)))
    run(u_copies)
    join(g_copies)
    total = g_ref[2 * y_bit + z_bit].astype(F32)
    for k in range(3):
        total = total + gr[k].astype(F32)
    gx_ref[...] = total.astype(BF16)
    join(u_copies)
    h_copies = []
    for d in (4, 3, 5, 2, 6, 1, 7):
        h_copies.append(remote(u, h_ref.at[gy], hsend.at[d - 1], hrecv.at[d - 1], ring("gy", gy, d)))
    run(h_copies)
    h_ref[gy] = u[...]
    join(h_copies)


def vmem(count):
    return [pl.BlockSpec(memory_space=pltpu.VMEM)] * count


def dma(*shape):
    return pltpu.SemaphoreType.DMA(shape)


def call(kernel, number, shapes, scratch, *operands):
    return pl.pallas_call(
        kernel,
        out_shape=[jax.ShapeDtypeStruct(shape, BF16) for shape in shapes],
        in_specs=vmem(len(operands)),
        out_specs=vmem(len(shapes)),
        scratch_shapes=scratch,
        compiler_params=pltpu.CompilerParams(collective_id=number, has_side_effects=True),
    )(*operands)


def transpose_dot(left, right):
    return lax.dot_general(left, right, (((1,), (1,)), ((), ())), preferred_element_type=F32)


def token_dot(left, right):
    return lax.dot_general(left, right, (((0,), (0,)), ((), ())), preferred_element_type=F32)


def dot(left, right):
    return jnp.dot(left, right, preferred_element_type=F32)


def on_device(features, grad_y, attn_out, w_query, w_key, w_value, w_out):
    width = features.shape[3]
    local = features.shape[0] * features.shape[1] * features.shape[2]
    tokens = 4 * local
    quarter = width // 4
    feature_rows = features.reshape(local, width)
    dy_rows = grad_y.reshape(local, width)
    saved_rows = attn_out.reshape(local, width)
    fb, gb, ab, w3, wo = call(
        gather_kernel,
        0,
        [(4, local, width)] * 3 + [(3, width, quarter), (quarter, width)],
        [dma(3, 3), dma(3, 3), dma(7, 3), dma(7, 3), dma(4), dma(2)],
        feature_rows, dy_rows, saved_rows, w_query, w_key, w_value, w_out,
    )
    fb, gb, ab = (block.reshape(tokens, width) for block in (fb, gb, ab))
    start = (lax.axis_index("gz") % 2) * (2 * quarter) + (lax.axis_index("gy") % 2) * quarter
    own_gb = lax.dynamic_slice_in_dim(gb, start, quarter, 1)
    own_ab = lax.dynamic_slice_in_dim(ab, start, quarter, 1)
    query, key, value = (dot(fb, w3[i]).astype(BF16) for i in range(3))
    grad = transpose_dot(gb, wo).astype(BF16)
    own_pair = jnp.stack([key, value])
    products = grad.astype(F32) * own_ab.astype(F32)
    row_delta = jnp.sum(products.reshape(tokens, 2, quarter // 2), axis=2).T.reshape(1, 2 * tokens)
    query_grad, pair_grads = call(
        attend_kernel,
        1,
        [(tokens, quarter), (2, tokens, quarter)],
        [
            pltpu.VMEM((7, 2, tokens, quarter), BF16),
            pltpu.VMEM((7, tokens, 2 * tokens), F32),
            pltpu.VMEM((7, 2, tokens, quarter), BF16),
            pltpu.VMEM((7, 2, tokens, quarter), BF16),
            pltpu.VMEM((quarter, 2 * tokens), BF16),
            pltpu.VMEM((quarter, 2 * tokens), BF16),
            pltpu.VMEM((quarter, tokens), BF16),
            pltpu.VMEM((2 * tokens, quarter), BF16),
            pltpu.VMEM((2 * tokens, quarter), BF16),
            pltpu.VMEM((tokens, 2 * tokens), BF16),
            pltpu.VMEM((tokens, 2 * tokens), BF16),
            pltpu.VMEM((quarter, 2 * tokens), F32),
            pltpu.VMEM((1, 2 * tokens), F32),
            pltpu.VMEM((1, 2 * tokens), F32),
            dma(2, 7), dma(2, 7), dma(7), dma(7),
        ],
        query, grad, row_delta, own_pair,
    )
    grads = (query_grad, pair_grads[0], pair_grads[1])
    partial_x = sum(transpose_dot(grads[i], w3[i]) for i in range(3))
    partial_x = partial_x.astype(BF16).reshape(4, local, width)
    terms = jnp.stack([token_dot(fb, part) for part in grads] + [token_dot(ab, own_gb)])
    terms = terms.astype(BF16).reshape(4, 8, 8, 8, quarter).transpose(0, 2, 1, 3, 4)
    terms = terms.reshape(4, 8, 64, quarter)
    rows, grad_x = call(
        reduce_kernel,
        2,
        [(8, 8, 16, quarter), (local, width)],
        [
            pltpu.VMEM((3, 8, 64, quarter), BF16),
            pltpu.VMEM((8, 64, quarter), BF16),
            pltpu.VMEM((7, 64, quarter), BF16),
            pltpu.VMEM((8, 8, quarter), F32),
            pltpu.VMEM((8, 8, quarter), F32),
            pltpu.VMEM((8, 16, quarter), BF16),
            pltpu.VMEM((3, local, width), BF16),
            dma(3), dma(3), dma(7), dma(7), dma(7), dma(7), dma(7), dma(7), dma(7), dma(7), dma(3), dma(3),
        ],
        terms, partial_x,
    )
    rows = rows.astype(F32).reshape(4, 2, 8, 2, 8, quarter).transpose(0, 2, 4, 3, 1, 5).reshape(4, 64, width)
    return (grad_x.reshape(features.shape), rows[0], rows[1], rows[2], rows[3])


def solution(mesh):
    token_spec = P("gx", "gy", "gz", None)
    row_spec = P("gz", None)
    return jax.shard_map(
        on_device,
        mesh=mesh,
        in_specs=(token_spec,) * 3 + (row_spec,) * 4,
        out_specs=(token_spec,) + (row_spec,) * 4,
        check_vma=False,
    )
```

```python
import jax
import jax.numpy as jnp
from jax import lax
from jax.experimental import pallas as pl
from jax.experimental.pallas import tpu as pltpu
from jax.sharding import PartitionSpec as P

HEADS = 8
MESH = pl.DeviceIdType.MESH
STEPS = (("gx", 1), ("gx", -1), ("gy", 2), ("gy", -2), ("gz", 2), ("gz", -2))
BF16 = jnp.bfloat16
F32 = jnp.float32


def remote(src, dst, send, recv, device):
    return pltpu.make_async_remote_copy(
        src_ref=src, dst_ref=dst, send_sem=send, recv_sem=recv, device_id=device, device_id_type=MESH
    )


def greet(devices):
    barrier = pltpu.get_barrier_semaphore()
    for device in devices:
        pl.semaphore_signal(barrier, inc=1, device_id=device, device_id_type=MESH)
    pl.semaphore_wait(barrier, len(devices))


def ring(axis, index, step):
    return {axis: lax.rem(index + step + 8, 8)}


def block_kernel(
    f_ref, g_ref, a_ref, wq_ref, wk_ref, wv_ref, wo_ref,
    fb_ref, ab_ref, gown_ref, w3_ref, dq_ref, dkv_ref,
    gb_ref, wob_ref, own_ref, delta_ref,
    kv, scores, part, back, qt, gt, kt, qs, gs, prob, grad, dqt, top, total,
    rsend, rrecv, wsend, wrecv, osend, orecv,
    ksend, krecv, bsend, brecv,
):
    index = {axis: lax.axis_index(axis) for axis in ("gx", "gy", "gz")}
    gy, gz = index["gy"], index["gz"]
    tokens, width = dq_ref.shape
    local = f_ref.shape[0]
    chunk = tokens // 2
    y_bit, z_bit = lax.rem(gy, 2), lax.rem(gz, 2)
    pair_z = {"gz": gz + 1 - 2 * z_bit}
    pair_y = {"gy": gy + 1 - 2 * y_bit}
    own_columns = pl.ds(pl.multiple_of(z_bit * 256 + y_bit * 128, 128), 128)
    greet(
        [ring("gz", gz, d) for d in range(1, 8)]
        + [pair_y]
        + [ring(axis, index[axis], step) for axis, step in STEPS[:4]]
    )

    def slot_rows(slot):
        return pl.ds(pl.multiple_of(slot * local, local), local)

    mine = slot_rows(2 * y_bit + z_bit)
    theirs = slot_rows(2 * (1 - y_bit) + z_bit)
    trios = ((f_ref, fb_ref), (g_ref, gb_ref), (a_ref, ab_ref))
    to_y = [remote(src, dst.at[mine], rsend.at[0, i], rrecv.at[0, i], pair_y) for i, (src, dst) in enumerate(trios)]
    to_z = [remote(src, dst.at[mine], rsend.at[1, i], rrecv.at[1, i], pair_z) for i, (src, dst) in enumerate(trios)]
    onward = [
        remote(dst.at[theirs], dst.at[theirs], rsend.at[2, i], rrecv.at[2, i], pair_z)
        for i, (src, dst) in enumerate(trios)
    ]
    weights = (wq_ref, wk_ref, wv_ref)
    weight_rows = pl.ds(pl.multiple_of(gz * 64, 64), 64)

    def weight_copy(i, d):
        target = lax.rem(gz + d, 8)
        columns = pl.ds(pl.multiple_of(lax.rem(target, 2) * 256 + y_bit * 128, 128), 128)
        return remote(
            weights[i].at[:, columns], w3_ref.at[i, weight_rows], wsend.at[d - 1, i], wrecv.at[d - 1, i], {"gz": target}
        )

    half = lax.rem(gz, 2)
    out_core = lax.div(gz, 4)
    out_from = lax.rem(lax.div(gz, 2), 2) == y_bit
    out_rows = pl.ds(pl.multiple_of(half * 64, 64), 64)

    def out_copy(zh):
        return remote(wo_ref, wob_ref.at[out_rows], osend.at[zh], orecv.at[half], {"gz": 2 * zh + out_core})

    def begin_share(i):
        to_y[i].start()
        to_z[i].start()
        src, dst = trios[i]
        dst[mine] = src[...]

    def pass_on(i):
        to_y[i].wait_recv()
        onward[i].start()

    def end_share(i):
        to_z[i].wait_recv()
        onward[i].wait_recv()

    order = (4, 3, 5, 2, 6, 1, 7)
    begin_share(0)
    for i in (1, 0, 2):
        for d in order:
            weight_copy(i, d).start()
        w3_ref[i, weight_rows] = weights[i][:, own_columns]
    begin_share(1)
    pass_on(0)
    end_share(0)

    def project(i):
        for d in order:
            weight_copy(i, d).wait_recv()
        return dot(fb_ref[...], w3_ref[i])

    def outward(i, k):
        axis, step = STEPS[k]
        return remote(own_ref.at[i], kv.at[k + 1, i], ksend.at[i, k + 1], krecv.at[i, k + 1], ring(axis, index[axis], step))

    def homeward(slot):
        pair = lax.div(slot - 1, 2)
        sign = 1 - 2 * lax.rem(slot - 1, 2)
        at_z = lax.div(pair, 2)
        at_y = pair - 2 * at_z
        at_x = 1 - at_y - at_z
        device = {
            "gx": lax.rem(index["gx"] - at_x * sign + 8, 8),
            "gy": lax.rem(index["gy"] - 2 * at_y * sign + 8, 8),
            "gz": lax.rem(index["gz"] - 2 * at_z * sign + 8, 8),
        }
        return remote(part.at[slot], back.at[slot], bsend.at[slot], brecv.at[slot], device)

    row_head = lax.broadcasted_iota(jnp.int32, (width, tokens), 0) // (width // 2)
    lane_head = lax.broadcasted_iota(jnp.int32, (tokens, width), 1) // (width // 2)

    def spread(value, turned, stacked):
        flipped = value.T
        for head in range(2):
            turned[:, head * tokens : (head + 1) * tokens] = jnp.where(row_head == head, flipped, 0.0).astype(BF16)
            stacked[head * tokens : (head + 1) * tokens, :] = jnp.where(lane_head == head, value, 0.0).astype(BF16)

    def send_own(i, w):
        value = project(w).astype(BF16)
        own_ref[i] = value
        kv[0, i] = value
        for k in (4, 5, 0, 1, 2, 3):
            outward(i, k).start()

    send_own(0, 1)
    for zh in range(4):

        @pl.when(jnp.logical_and(out_from, 2 * zh + out_core != gz))
        def _():
            out_copy(zh).start()

    begin_share(2)
    send_own(1, 2)
    pass_on(1)
    spread(project(0).astype(BF16).astype(F32) * 0.125, qt, qs)
    top[...] = jnp.full_like(top, -jnp.inf)
    total[...] = jnp.zeros_like(total)
    dqt[...] = jnp.zeros_like(dqt)
    pass_on(2)

    def arrived(i, slot):
        return remote(own_ref.at[i], kv.at[slot, i], ksend.at[i, slot], krecv.at[i, slot], ring("gx", index["gx"], 1))

    def first_pass(slot, unused):
        @pl.when(slot > 0)
        def _():
            arrived(0, slot).wait_recv()

        for c in range(4):
            columns = slice(c * chunk, (c + 1) * chunk)
            block = dot(kv[slot, 0], qt[:, columns])
            scores[slot, :, columns] = block
            old_top = top[:, columns]
            new_top = jnp.maximum(old_top, jnp.max(block, axis=0, keepdims=True))
            summed = jnp.sum(jnp.exp(block - new_top), axis=0, keepdims=True)
            total[:, columns] = total[:, columns] * jnp.exp(old_top - new_top) + summed
            top[:, columns] = new_top
        return unused

    lax.fori_loop(0, 7, first_pass, 0)
    top[...] = top[...] + jnp.log(total[...])
    for s in range(2):
        source = 4 * z_bit + 2 * y_bit + s

        @pl.when(source != gz)
        def _():
            remote(wo_ref, wob_ref.at[pl.ds(s * 64, 64)], osend.at[0], orecv.at[s], {"gz": source}).wait_recv()

        @pl.when(source == gz)
        def _():
            wob_ref[pl.ds(s * 64, 64)] = wo_ref[...]

    end_share(1)
    end_share(2)
    gown_ref[...] = gb_ref[:, own_columns]
    upstream = transpose_dot(gb_ref[...], wob_ref[...]).astype(BF16).astype(F32)
    spread(upstream, gt, gs)
    products = (upstream * ab_ref[:, own_columns].astype(F32)).T
    for head in range(2):
        rows = products[head * (width // 2) : (head + 1) * (width // 2)]
        delta_ref[:, head * tokens : (head + 1) * tokens] = jnp.sum(rows, axis=0, keepdims=True)

    def second_pass(turn, unused):
        last = lax.div(turn, 6)
        group = lax.div(turn, 2)
        slot = (1 + 2 * (2 * group - 3 * lax.div(group, 2)) + lax.rem(turn, 2)) * (1 - last)

        @pl.when(turn < 6)
        def _():
            arrived(1, slot).wait_recv()

        kt[...] = kv[slot, 0].astype(F32).T.astype(BF16)
        for c in range(4):
            columns = slice(c * chunk, (c + 1) * chunk)
            p = jnp.exp(scores[slot, :, columns] - top[:, columns]).astype(BF16)
            prob[:, columns] = p
            dp = dot(kv[slot, 1], gt[:, columns])
            ds = (p.astype(F32) * (dp - delta_ref[:, columns])).astype(BF16)
            grad[:, columns] = ds
            dqt[:, columns] += dot(kt[...], ds)
        part[slot, 0] = dot(grad[...], qs[...]).astype(BF16)
        part[slot, 1] = dot(prob[...], gs[...]).astype(BF16)

        @pl.when(turn < 6)
        def _():
            homeward(slot).start()

        return unused

    lax.fori_loop(0, 7, second_pass, 0)
    middle = width // 2
    turned = jnp.concatenate([dqt[:middle, :tokens], dqt[middle:, tokens:]], axis=0) * 0.125
    dq_ref[...] = turned.T.astype(BF16)
    for i in range(3):
        to_y[i].wait_send()
        to_z[i].wait_send()
        onward[i].wait_send()
        for d in order:
            weight_copy(i, d).wait_send()
    for zh in range(4):

        @pl.when(jnp.logical_and(out_from, 2 * zh + out_core != gz))
        def _():
            out_copy(zh).wait_send()

    for i in range(2):
        for k in range(6):
            outward(i, k).wait_send()
    for slot in (1, 2, 5, 6, 3, 4):
        homeward(slot).wait()
    for i in range(2):
        whole = part[0, i].astype(F32)
        for slot in range(1, 7):
            whole = whole + back[slot, i].astype(F32)
        dkv_ref[i] = whole.astype(BF16)


def reduce_kernel(
    t_ref, g_ref, h_ref, gx_ref,
    xr, s1, yr, s2, zr, u, gr,
    xsend, xrecv, ysend, yrecv, zsend, zrecv, usend, urecv, hsend, hrecv, gsend, grecv,
):
    gx, gy, gz = (lax.axis_index(axis) for axis in ("gx", "gy", "gz"))
    y_bit, z_bit = lax.rem(gy, 2), lax.rem(gz, 2)
    x = lax.div(gy, 2)
    other_z, other_y = gz + 1 - 2 * z_bit, gy + 1 - 2 * y_bit
    greet(
        [ring("gy", gy, d) for d in range(1, 8)]
        + [ring("gx", gx, d) for d in range(1, 8)]
        + [ring("gz", gz, d) for d in range(1, 8)]
        + [{"gy": other_y, "gz": other_z}]
    )

    def run(copies):
        for copy in copies:
            copy.start()
        return copies

    def join(copies):
        for copy in copies:
            copy.wait()

    x_copies = []
    for d in (2, 1, 3):
        target = lax.rem(x + d, 4)
        x_copies.append(
            remote(t_ref.at[target], xr.at[d - 1], xsend.at[d - 1], xrecv.at[d - 1], {"gy": 2 * target + y_bit})
        )
    run(x_copies)
    parts = (
        (2 * (1 - y_bit) + 1 - z_bit, {"gy": other_y, "gz": other_z}),
        (2 * (1 - y_bit) + z_bit, {"gy": other_y}),
        (2 * y_bit + 1 - z_bit, {"gz": other_z}),
    )
    g_copies = run(
        [remote(g_ref.at[part], gr.at[k], gsend.at[k], grecv.at[k], dev) for k, (part, dev) in enumerate(parts)]
    )
    join(x_copies)
    total = t_ref[x].astype(F32)
    for d in range(3):
        total = total + xr[d].astype(F32)
    s1[...] = total.astype(BF16)
    y_copies = []
    for d in (4, 3, 5, 2, 6, 1, 7):
        target = lax.rem(gx + d, 8)
        y_copies.append(remote(s1.at[target], yr.at[d - 1], ysend.at[d - 1], yrecv.at[d - 1], {"gx": target}))
    run(y_copies)
    join(y_copies)
    total = s1[gx].astype(F32)
    for d in range(7):
        total = total + yr[d].astype(F32)
    s2[...] = total.reshape(8, 8, 128)
    z_copies = []
    for d in (4, 3, 5, 2, 6, 1, 7):
        target = lax.rem(gz + d, 8)
        z_copies.append(remote(s2.at[target], zr.at[gz], zsend.at[d - 1], zrecv.at[d - 1], {"gz": target}))
    run(z_copies)
    zr[gz] = s2[gz]
    join(z_copies)
    lower = zr[0] + zr[2] + zr[4] + zr[6]
    upper = zr[1] + zr[3] + zr[5] + zr[7]
    u[gx] = jnp.concatenate([lower, upper], axis=0).astype(BF16)
    u_copies = []
    for d in (4, 3, 5, 2, 6, 1, 7):
        u_copies.append(remote(u.at[gx], u.at[gx], usend.at[d - 1], urecv.at[d - 1], ring("gx", gx, d)))
    run(u_copies)
    join(g_copies)
    total = g_ref[2 * y_bit + z_bit].astype(F32)
    for k in range(3):
        total = total + gr[k].astype(F32)
    gx_ref[...] = total.astype(BF16)
    join(u_copies)
    h_copies = []
    for d in (4, 3, 5, 2, 6, 1, 7):
        h_copies.append(remote(u, h_ref.at[gy], hsend.at[d - 1], hrecv.at[d - 1], ring("gy", gy, d)))
    run(h_copies)
    h_ref[gy] = u[...]
    join(h_copies)


def vmem(count):
    return [pl.BlockSpec(memory_space=pltpu.VMEM)] * count


def dma(*shape):
    return pltpu.SemaphoreType.DMA(shape)


def call(kernel, number, shapes, scratch, *operands):
    return pl.pallas_call(
        kernel,
        out_shape=[jax.ShapeDtypeStruct(shape, BF16) for shape in shapes],
        in_specs=vmem(len(operands)),
        out_specs=vmem(len(shapes)),
        scratch_shapes=scratch,
        compiler_params=pltpu.CompilerParams(collective_id=number, has_side_effects=True),
    )(*operands)


def transpose_dot(left, right):
    return lax.dot_general(left, right, (((1,), (1,)), ((), ())), preferred_element_type=F32)


def token_dot(left, right):
    return lax.dot_general(left, right, (((0,), (0,)), ((), ())), preferred_element_type=F32)


def dot(left, right):
    return jnp.dot(left, right, preferred_element_type=F32)


def on_device(features, grad_y, attn_out, w_query, w_key, w_value, w_out):
    width = features.shape[3]
    local = features.shape[0] * features.shape[1] * features.shape[2]
    tokens = 4 * local
    quarter = width // 4
    feature_rows = features.reshape(local, width)
    dy_rows = grad_y.reshape(local, width)
    saved_rows = attn_out.reshape(local, width)
    fb, ab, own_gb, w3, query_grad, pair_grads = call(
        block_kernel,
        0,
        [(tokens, width), (tokens, width), (tokens, quarter), (3, width, quarter), (tokens, quarter), (2, tokens, quarter)],
        [
            pltpu.VMEM((tokens, width), BF16),
            pltpu.VMEM((quarter, width), BF16),
            pltpu.VMEM((2, tokens, quarter), BF16),
            pltpu.VMEM((1, 2 * tokens), F32),
            pltpu.VMEM((7, 2, tokens, quarter), BF16),
            pltpu.VMEM((7, tokens, 2 * tokens), F32),
            pltpu.VMEM((7, 2, tokens, quarter), BF16),
            pltpu.VMEM((7, 2, tokens, quarter), BF16),
            pltpu.VMEM((quarter, 2 * tokens), BF16),
            pltpu.VMEM((quarter, 2 * tokens), BF16),
            pltpu.VMEM((quarter, tokens), BF16),
            pltpu.VMEM((2 * tokens, quarter), BF16),
            pltpu.VMEM((2 * tokens, quarter), BF16),
            pltpu.VMEM((tokens, 2 * tokens), BF16),
            pltpu.VMEM((tokens, 2 * tokens), BF16),
            pltpu.VMEM((quarter, 2 * tokens), F32),
            pltpu.VMEM((1, 2 * tokens), F32),
            pltpu.VMEM((1, 2 * tokens), F32),
            dma(3, 3), dma(3, 3), dma(7, 3), dma(7, 3), dma(4), dma(2),
            dma(2, 7), dma(2, 7), dma(7), dma(7),
        ],
        feature_rows, dy_rows, saved_rows, w_query, w_key, w_value, w_out,
    )
    grads = (query_grad, pair_grads[0], pair_grads[1])
    partial_x = sum(transpose_dot(grads[i], w3[i]) for i in range(3))
    partial_x = partial_x.astype(BF16).reshape(4, local, width)
    terms = jnp.stack([token_dot(fb, part) for part in grads] + [token_dot(ab, own_gb)])
    terms = terms.astype(BF16).reshape(4, 8, 8, 8, quarter).transpose(0, 2, 1, 3, 4)
    terms = terms.reshape(4, 8, 64, quarter)
    rows, grad_x = call(
        reduce_kernel,
        1,
        [(8, 8, 16, quarter), (local, width)],
        [
            pltpu.VMEM((3, 8, 64, quarter), BF16),
            pltpu.VMEM((8, 64, quarter), BF16),
            pltpu.VMEM((7, 64, quarter), BF16),
            pltpu.VMEM((8, 8, quarter), F32),
            pltpu.VMEM((8, 8, quarter), F32),
            pltpu.VMEM((8, 16, quarter), BF16),
            pltpu.VMEM((3, local, width), BF16),
            dma(3), dma(3), dma(7), dma(7), dma(7), dma(7), dma(7), dma(7), dma(7), dma(7), dma(3), dma(3),
        ],
        terms, partial_x,
    )
    rows = rows.astype(F32).reshape(4, 2, 8, 2, 8, quarter).transpose(0, 2, 4, 3, 1, 5).reshape(4, 64, width)
    return (grad_x.reshape(features.shape), rows[0], rows[1], rows[2], rows[3])


def solution(mesh):
    token_spec = P("gx", "gy", "gz", None)
    row_spec = P("gz", None)
    return jax.shard_map(
        on_device,
        mesh=mesh,
        in_specs=(token_spec,) * 3 + (row_spec,) * 4,
        out_specs=(token_spec,) + (row_spec,) * 4,
        check_vma=False,
    )
```

```python
import jax
import jax.numpy as jnp
from jax import lax
from jax.experimental import pallas as pl
from jax.experimental.pallas import tpu as pltpu
from jax.sharding import PartitionSpec as P

HEADS = 8
MESH = pl.DeviceIdType.MESH
STEPS = (("gx", 1), ("gx", -1), ("gy", 2), ("gy", -2), ("gz", 2), ("gz", -2))
BF16 = jnp.bfloat16
F32 = jnp.float32


def remote(src, dst, send, recv, device):
    return pltpu.make_async_remote_copy(
        src_ref=src, dst_ref=dst, send_sem=send, recv_sem=recv, device_id=device, device_id_type=MESH
    )


def greet(devices):
    barrier = pltpu.get_barrier_semaphore()
    for device in devices:
        pl.semaphore_signal(barrier, inc=1, device_id=device, device_id_type=MESH)
    pl.semaphore_wait(barrier, len(devices))


def ring(axis, index, step):
    return {axis: lax.rem(index + step + 8, 8)}


def block_kernel(
    f_ref, g_ref, a_ref, wq_ref, wk_ref, wv_ref, wo_ref,
    h_ref, gx_ref,
    fb_ref, ab_ref, gown_ref, w3_ref, ft, at,
    gb_ref, wob_ref, own_ref, delta_ref,
    kv, scores, part, back, qt, gt, kt, qs, gs, prob, grad, dqt, top, total,
    terms, partial_x, xr, s1, yr, s2, zr, u, gr,
    rsend, rrecv, wsend, wrecv, osend, orecv,
    ksend, krecv, bsend, brecv,
    xsend, xrecv, ysend, yrecv, zsend, zrecv, usend, urecv, hsend, hrecv, gsend, grecv,
):
    index = {axis: lax.axis_index(axis) for axis in ("gx", "gy", "gz")}
    gx, gy, gz = index["gx"], index["gy"], index["gz"]
    tokens, width = gown_ref.shape
    local = f_ref.shape[0]
    chunk = tokens // 2
    y_bit, z_bit = lax.rem(gy, 2), lax.rem(gz, 2)
    pair_z = {"gz": gz + 1 - 2 * z_bit}
    pair_y = {"gy": gy + 1 - 2 * y_bit}
    own_columns = pl.ds(pl.multiple_of(z_bit * 256 + y_bit * 128, 128), 128)
    pair_both = {"gy": pair_y["gy"], "gz": pair_z["gz"]}
    x = lax.div(gy, 2)
    greet([ring(axis, index[axis], d) for axis in ("gx", "gy", "gz") for d in range(1, 8)] + [pair_both])

    def slot_rows(slot):
        return pl.ds(pl.multiple_of(slot * local, local), local)

    mine = slot_rows(2 * y_bit + z_bit)
    theirs = slot_rows(2 * (1 - y_bit) + z_bit)
    trios = ((f_ref, fb_ref), (g_ref, gb_ref), (a_ref, ab_ref))
    to_y = [remote(src, dst.at[mine], rsend.at[0, i], rrecv.at[0, i], pair_y) for i, (src, dst) in enumerate(trios)]
    to_z = [remote(src, dst.at[mine], rsend.at[1, i], rrecv.at[1, i], pair_z) for i, (src, dst) in enumerate(trios)]
    onward = [
        remote(dst.at[theirs], dst.at[theirs], rsend.at[2, i], rrecv.at[2, i], pair_z)
        for i, (src, dst) in enumerate(trios)
    ]
    weights = (wq_ref, wk_ref, wv_ref)
    weight_rows = pl.ds(pl.multiple_of(gz * 64, 64), 64)

    def weight_copy(i, d):
        target = lax.rem(gz + d, 8)
        columns = pl.ds(pl.multiple_of(lax.rem(target, 2) * 256 + y_bit * 128, 128), 128)
        return remote(
            weights[i].at[:, columns], w3_ref.at[i, weight_rows], wsend.at[d - 1, i], wrecv.at[d - 1, i], {"gz": target}
        )

    half = lax.rem(gz, 2)
    out_core = lax.div(gz, 4)
    out_from = lax.rem(lax.div(gz, 2), 2) == y_bit
    out_rows = pl.ds(pl.multiple_of(half * 64, 64), 64)

    def out_copy(zh):
        return remote(wo_ref, wob_ref.at[out_rows], osend.at[zh], orecv.at[half], {"gz": 2 * zh + out_core})

    def begin_share(i):
        to_y[i].start()
        to_z[i].start()
        src, dst = trios[i]
        dst[mine] = src[...]

    def pass_on(i):
        to_y[i].wait_recv()
        onward[i].start()

    def end_share(i):
        to_z[i].wait_recv()
        onward[i].wait_recv()

    order = (4, 3, 5, 2, 6, 1, 7)
    begin_share(0)
    for i in (1, 0, 2):
        for d in order:
            weight_copy(i, d).start()
        w3_ref[i, weight_rows] = weights[i][:, own_columns]
    begin_share(1)
    pass_on(0)
    end_share(0)

    def project(i):
        for d in order:
            weight_copy(i, d).wait_recv()
        return dot(fb_ref[...], w3_ref[i])

    def outward(i, k):
        axis, step = STEPS[k]
        return remote(own_ref.at[i], kv.at[k + 1, i], ksend.at[i, k + 1], krecv.at[i, k + 1], ring(axis, index[axis], step))

    def homeward(slot):
        pair = lax.div(slot - 1, 2)
        sign = 1 - 2 * lax.rem(slot - 1, 2)
        at_z = lax.div(pair, 2)
        at_y = pair - 2 * at_z
        at_x = 1 - at_y - at_z
        device = {
            "gx": lax.rem(index["gx"] - at_x * sign + 8, 8),
            "gy": lax.rem(index["gy"] - 2 * at_y * sign + 8, 8),
            "gz": lax.rem(index["gz"] - 2 * at_z * sign + 8, 8),
        }
        return remote(part.at[slot], back.at[slot], bsend.at[slot], brecv.at[slot], device)

    row_head = lax.broadcasted_iota(jnp.int32, (width, tokens), 0) // (width // 2)
    lane_head = lax.broadcasted_iota(jnp.int32, (tokens, width), 1) // (width // 2)

    def spread(value, turned, stacked):
        flipped = value.T
        for head in range(2):
            turned[:, head * tokens : (head + 1) * tokens] = jnp.where(row_head == head, flipped, 0.0).astype(BF16)
            stacked[head * tokens : (head + 1) * tokens, :] = jnp.where(lane_head == head, value, 0.0).astype(BF16)

    def send_own(i, w):
        value = project(w).astype(BF16)
        own_ref[i] = value
        kv[0, i] = value
        for k in (4, 5, 0, 1, 2, 3):
            outward(i, k).start()

    def reduce_x(m, d):
        target = lax.rem(x + d, 4)
        return remote(
            terms.at[target, pl.ds(2 * m, 2)], xr.at[d - 1, pl.ds(2 * m, 2)],
            xsend.at[d - 1, m], xrecv.at[d - 1, m], {"gy": 2 * target + y_bit},
        )

    def begin_term(m, term):
        split = term.reshape(8, 8, 8, width)
        for group in range(8):
            terms[group // 2, 2 * m + group % 2] = split[:, group].reshape(64, width).astype(BF16)
        for d in (2, 1, 3):
            reduce_x(m, d).start()

    send_own(0, 1)
    for zh in range(4):

        @pl.when(jnp.logical_and(out_from, 2 * zh + out_core != gz))
        def _():
            out_copy(zh).start()

    begin_share(2)
    send_own(1, 2)
    pass_on(1)
    spread(project(0).astype(BF16).astype(F32) * 0.125, qt, qs)
    top[...] = jnp.full_like(top, -jnp.inf)
    total[...] = jnp.zeros_like(total)
    dqt[...] = jnp.zeros_like(dqt)
    pass_on(2)
    ft[...] = fb_ref[...].astype(F32).T.astype(BF16)

    def arrived(i, slot):
        return remote(own_ref.at[i], kv.at[slot, i], ksend.at[i, slot], krecv.at[i, slot], ring("gx", index["gx"], 1))

    def first_pass(slot, unused):
        @pl.when(slot > 0)
        def _():
            arrived(0, slot).wait_recv()

        for c in range(4):
            columns = slice(c * chunk, (c + 1) * chunk)
            block = dot(kv[slot, 0], qt[:, columns])
            scores[slot, :, columns] = block
            old_top = top[:, columns]
            new_top = jnp.maximum(old_top, jnp.max(block, axis=0, keepdims=True))
            summed = jnp.sum(jnp.exp(block - new_top), axis=0, keepdims=True)
            total[:, columns] = total[:, columns] * jnp.exp(old_top - new_top) + summed
            top[:, columns] = new_top
        return unused

    lax.fori_loop(0, 7, first_pass, 0)
    top[...] = top[...] + jnp.log(total[...])
    for s in range(2):
        source = 4 * z_bit + 2 * y_bit + s

        @pl.when(source != gz)
        def _():
            remote(wo_ref, wob_ref.at[pl.ds(s * 64, 64)], osend.at[0], orecv.at[s], {"gz": source}).wait_recv()

        @pl.when(source == gz)
        def _():
            wob_ref[pl.ds(s * 64, 64)] = wo_ref[...]

    end_share(1)
    end_share(2)
    gown_ref[...] = gb_ref[:, own_columns]
    upstream = transpose_dot(gb_ref[...], wob_ref[...]).astype(BF16).astype(F32)
    spread(upstream, gt, gs)
    products = (upstream * ab_ref[:, own_columns].astype(F32)).T
    for head in range(2):
        rows = products[head * (width // 2) : (head + 1) * (width // 2)]
        delta_ref[:, head * tokens : (head + 1) * tokens] = jnp.sum(rows, axis=0, keepdims=True)

    at[...] = ab_ref[...].astype(F32).T.astype(BF16)
    begin_term(3, dot(at[...], gown_ref[...]))

    def second_pass(turn, unused):
        last = lax.div(turn, 6)
        group = lax.div(turn, 2)
        slot = (1 + 2 * (2 * group - 3 * lax.div(group, 2)) + lax.rem(turn, 2)) * (1 - last)

        @pl.when(turn < 6)
        def _():
            arrived(1, slot).wait_recv()

        kt[...] = kv[slot, 0].astype(F32).T.astype(BF16)
        for c in range(4):
            columns = slice(c * chunk, (c + 1) * chunk)
            p = jnp.exp(scores[slot, :, columns] - top[:, columns]).astype(BF16)
            prob[:, columns] = p
            dp = dot(kv[slot, 1], gt[:, columns])
            ds = (p.astype(F32) * (dp - delta_ref[:, columns])).astype(BF16)
            grad[:, columns] = ds
            dqt[:, columns] += dot(kt[...], ds)
        part[slot, 0] = dot(grad[...], qs[...]).astype(BF16)
        part[slot, 1] = dot(prob[...], gs[...]).astype(BF16)

        @pl.when(turn < 6)
        def _():
            homeward(slot).start()

        return unused

    lax.fori_loop(0, 7, second_pass, 0)
    middle = width // 2
    turned = jnp.concatenate([dqt[:middle, :tokens], dqt[middle:, tokens:]], axis=0) * 0.125
    dq = turned.T.astype(BF16)
    begin_term(0, dot(ft[...], dq))
    across = transpose_dot(dq, w3_ref[0])
    for i in range(3):
        to_y[i].wait_send()
        to_z[i].wait_send()
        onward[i].wait_send()
        for d in order:
            weight_copy(i, d).wait_send()
    for zh in range(4):

        @pl.when(jnp.logical_and(out_from, 2 * zh + out_core != gz))
        def _():
            out_copy(zh).wait_send()

    for i in range(2):
        for k in range(6):
            outward(i, k).wait_send()
    for slot in (1, 2, 5, 6, 3, 4):
        homeward(slot).wait()
    for i in range(2):
        whole = part[0, i].astype(F32)
        for slot in range(1, 7):
            whole = whole + back[slot, i].astype(F32)
        pair_grad = whole.astype(BF16)
        begin_term(1 + i, dot(ft[...], pair_grad))
        across = across + transpose_dot(pair_grad, w3_ref[1 + i])
    partial_x[...] = across.astype(BF16)

    def join(copies):
        for copy in copies:
            copy.wait()

    def run(copies):
        for copy in copies:
            copy.start()

    owners = (
        (2 * (1 - y_bit) + 1 - z_bit, pair_both),
        (2 * (1 - y_bit) + z_bit, pair_y),
        (2 * y_bit + 1 - z_bit, pair_z),
    )
    g_copies = [
        remote(partial_x.at[slot_rows(slot)], gr.at[k], gsend.at[k], grecv.at[k], device)
        for k, (slot, device) in enumerate(owners)
    ]
    run(g_copies)
    for m in (3, 0, 1, 2):
        for d in (2, 1, 3):
            reduce_x(m, d).wait()
    whole = terms[x].astype(F32)
    for d in range(3):
        whole = whole + xr[d].astype(F32)
    s1[...] = whole.astype(BF16)
    y_copies = []
    for d in (4, 3, 5, 2, 6, 1, 7):
        target = lax.rem(gx + d, 8)
        y_copies.append(remote(s1.at[target], yr.at[d - 1], ysend.at[d - 1], yrecv.at[d - 1], {"gx": target}))
    run(y_copies)
    join(y_copies)
    whole = s1[gx].astype(F32)
    for d in range(7):
        whole = whole + yr[d].astype(F32)
    s2[...] = whole.reshape(8, 8, 128)
    z_copies = []
    for d in (4, 3, 5, 2, 6, 1, 7):
        target = lax.rem(gz + d, 8)
        z_copies.append(remote(s2.at[target], zr.at[gz], zsend.at[d - 1], zrecv.at[d - 1], {"gz": target}))
    run(z_copies)
    zr[gz] = s2[gz]
    join(z_copies)
    lower = zr[0] + zr[2] + zr[4] + zr[6]
    upper = zr[1] + zr[3] + zr[5] + zr[7]
    u[gx] = jnp.concatenate([lower, upper], axis=0).astype(BF16)
    u_copies = []
    for d in (4, 3, 5, 2, 6, 1, 7):
        u_copies.append(remote(u.at[gx], u.at[gx], usend.at[d - 1], urecv.at[d - 1], ring("gx", gx, d)))
    run(u_copies)
    join(g_copies)
    whole = partial_x[mine].astype(F32)
    for k in range(3):
        whole = whole + gr[k].astype(F32)
    gx_ref[...] = whole.astype(BF16)
    join(u_copies)
    h_copies = []
    for d in (4, 3, 5, 2, 6, 1, 7):
        h_copies.append(remote(u, h_ref.at[gy], hsend.at[d - 1], hrecv.at[d - 1], ring("gy", gy, d)))
    run(h_copies)
    h_ref[gy] = u[...]
    join(h_copies)


def vmem(count):
    return [pl.BlockSpec(memory_space=pltpu.VMEM)] * count


def dma(*shape):
    return pltpu.SemaphoreType.DMA(shape)


def call(kernel, number, shapes, scratch, *operands):
    return pl.pallas_call(
        kernel,
        out_shape=[jax.ShapeDtypeStruct(shape, BF16) for shape in shapes],
        in_specs=vmem(len(operands)),
        out_specs=vmem(len(shapes)),
        scratch_shapes=scratch,
        compiler_params=pltpu.CompilerParams(collective_id=number, has_side_effects=True),
    )(*operands)


def transpose_dot(left, right):
    return lax.dot_general(left, right, (((1,), (1,)), ((), ())), preferred_element_type=F32)


def dot(left, right):
    return jnp.dot(left, right, preferred_element_type=F32)


def on_device(features, grad_y, attn_out, w_query, w_key, w_value, w_out):
    width = features.shape[3]
    local = features.shape[0] * features.shape[1] * features.shape[2]
    tokens = 4 * local
    quarter = width // 4
    feature_rows = features.reshape(local, width)
    dy_rows = grad_y.reshape(local, width)
    saved_rows = attn_out.reshape(local, width)
    rows, grad_x = call(
        block_kernel,
        0,
        [(8, 8, 16, quarter), (local, width)],
        [
            pltpu.VMEM((tokens, width), BF16),
            pltpu.VMEM((tokens, width), BF16),
            pltpu.VMEM((tokens, quarter), BF16),
            pltpu.VMEM((3, width, quarter), BF16),
            pltpu.VMEM((width, tokens), BF16),
            pltpu.VMEM((width, tokens), BF16),
            pltpu.VMEM((tokens, width), BF16),
            pltpu.VMEM((quarter, width), BF16),
            pltpu.VMEM((2, tokens, quarter), BF16),
            pltpu.VMEM((1, 2 * tokens), F32),
            pltpu.VMEM((7, 2, tokens, quarter), BF16),
            pltpu.VMEM((7, tokens, 2 * tokens), F32),
            pltpu.VMEM((7, 2, tokens, quarter), BF16),
            pltpu.VMEM((7, 2, tokens, quarter), BF16),
            pltpu.VMEM((quarter, 2 * tokens), BF16),
            pltpu.VMEM((quarter, 2 * tokens), BF16),
            pltpu.VMEM((quarter, tokens), BF16),
            pltpu.VMEM((2 * tokens, quarter), BF16),
            pltpu.VMEM((2 * tokens, quarter), BF16),
            pltpu.VMEM((tokens, 2 * tokens), BF16),
            pltpu.VMEM((tokens, 2 * tokens), BF16),
            pltpu.VMEM((quarter, 2 * tokens), F32),
            pltpu.VMEM((1, 2 * tokens), F32),
            pltpu.VMEM((1, 2 * tokens), F32),
            pltpu.VMEM((4, 8, 64, quarter), BF16),
            pltpu.VMEM((tokens, width), BF16),
            pltpu.VMEM((3, 8, 64, quarter), BF16),
            pltpu.VMEM((8, 64, quarter), BF16),
            pltpu.VMEM((7, 64, quarter), BF16),
            pltpu.VMEM((8, 8, quarter), F32),
            pltpu.VMEM((8, 8, quarter), F32),
            pltpu.VMEM((8, 16, quarter), BF16),
            pltpu.VMEM((3, local, width), BF16),
            dma(3, 3), dma(3, 3), dma(7, 3), dma(7, 3), dma(4), dma(2),
            dma(2, 7), dma(2, 7), dma(7), dma(7),
            dma(3, 4), dma(3, 4), dma(7), dma(7), dma(7), dma(7), dma(7), dma(7), dma(7), dma(7), dma(3), dma(3),
        ],
        feature_rows, dy_rows, saved_rows, w_query, w_key, w_value, w_out,
    )
    rows = rows.astype(F32).reshape(4, 2, 4, 2, 2, 8, quarter).transpose(2, 0, 3, 5, 4, 1, 6).reshape(4, 64, width)
    return (grad_x.reshape(features.shape), rows[0], rows[1], rows[2], rows[3])


def solution(mesh):
    token_spec = P("gx", "gy", "gz", None)
    row_spec = P("gz", None)
    return jax.shard_map(
        on_device,
        mesh=mesh,
        in_specs=(token_spec,) * 3 + (row_spec,) * 4,
        out_specs=(token_spec,) + (row_spec,) * 4,
        check_vma=False,
    )
```

```python
import jax
import jax.numpy as jnp
from jax import lax
from jax.experimental import pallas as pl
from jax.experimental.pallas import tpu as pltpu
from jax.sharding import PartitionSpec as P

HEADS = 8
MESH = pl.DeviceIdType.MESH
STEPS = (("gx", 1), ("gx", -1), ("gy", 2), ("gy", -2), ("gz", 2), ("gz", -2))
BF16 = jnp.bfloat16
F32 = jnp.float32


def remote(src, dst, send, recv, device):
    return pltpu.make_async_remote_copy(
        src_ref=src, dst_ref=dst, send_sem=send, recv_sem=recv, device_id=device, device_id_type=MESH
    )


def greet(devices):
    barrier = pltpu.get_barrier_semaphore()
    for device in devices:
        pl.semaphore_signal(barrier, inc=1, device_id=device, device_id_type=MESH)
    pl.semaphore_wait(barrier, len(devices))


def ring(axis, index, step):
    return {axis: lax.rem(index + step + 8, 8)}


def block_kernel(
    f_in, g_in, a_in, wq_ref, wk_ref, wv_ref, wo_ref,
    h_ref, gx_ref,
    f_ref, g_ref, a_ref, stage,
    fb_ref, ab_ref, gown_ref, w3_ref, ft, at,
    gb_ref, wob_ref, own_ref, delta_ref,
    kv, scores, part, back, qt, gt, kt, qs, gs, prob, grad, dqt, top, total,
    terms, partial_x, xr, s1, yr, s2, zr, u, gr,
    rsend, rrecv, wsend, wrecv, osend, orecv,
    ksend, krecv, bsend, brecv,
    xsend, xrecv, ysend, yrecv, zsend, zrecv, usend, urecv, hsend, hrecv, gsend, grecv,
):
    index = {axis: lax.axis_index(axis) for axis in ("gx", "gy", "gz")}
    gx, gy, gz = index["gx"], index["gy"], index["gz"]
    tokens, width = gown_ref.shape
    local = f_ref.shape[0]
    chunk = tokens // 2
    y_bit, z_bit = lax.rem(gy, 2), lax.rem(gz, 2)
    pair_z = {"gz": gz + 1 - 2 * z_bit}
    pair_y = {"gy": gy + 1 - 2 * y_bit}
    own_columns = pl.ds(pl.multiple_of(z_bit * 256 + y_bit * 128, 128), 128)
    pair_both = {"gy": pair_y["gy"], "gz": pair_z["gz"]}
    x = lax.div(gy, 2)
    greet([ring(axis, index[axis], d) for axis in ("gx", "gy", "gz") for d in range(1, 8)] + [pair_both])

    def slot_rows(slot):
        return pl.ds(pl.multiple_of(slot * local, local), local)

    mine = slot_rows(2 * y_bit + z_bit)
    theirs = slot_rows(2 * (1 - y_bit) + z_bit)

    def flatten(source, target):
        for i in range(source.shape[0]):
            for j in range(4):
                stage[16 * i + 4 * j : 16 * i + 4 * j + 4] = source[i, j].astype(F32)
        target[...] = stage[...].astype(BF16)

    trios = ((f_ref, fb_ref), (g_ref, gb_ref), (a_ref, ab_ref))
    to_y = [remote(src, dst.at[mine], rsend.at[0, i], rrecv.at[0, i], pair_y) for i, (src, dst) in enumerate(trios)]
    to_z = [remote(src, dst.at[mine], rsend.at[1, i], rrecv.at[1, i], pair_z) for i, (src, dst) in enumerate(trios)]
    onward = [
        remote(dst.at[theirs], dst.at[theirs], rsend.at[2, i], rrecv.at[2, i], pair_z)
        for i, (src, dst) in enumerate(trios)
    ]
    weights = (wq_ref, wk_ref, wv_ref)
    weight_rows = pl.ds(pl.multiple_of(gz * 64, 64), 64)

    def weight_copy(i, d):
        target = lax.rem(gz + d, 8)
        columns = pl.ds(pl.multiple_of(lax.rem(target, 2) * 256 + y_bit * 128, 128), 128)
        return remote(
            weights[i].at[:, columns], w3_ref.at[i, weight_rows], wsend.at[d - 1, i], wrecv.at[d - 1, i], {"gz": target}
        )

    half = lax.rem(gz, 2)
    out_core = lax.div(gz, 4)
    out_from = lax.rem(lax.div(gz, 2), 2) == y_bit
    out_rows = pl.ds(pl.multiple_of(half * 64, 64), 64)

    def out_copy(zh):
        return remote(wo_ref, wob_ref.at[out_rows], osend.at[zh], orecv.at[half], {"gz": 2 * zh + out_core})

    def begin_share(i):
        flatten((f_in, g_in, a_in)[i], trios[i][0])
        to_y[i].start()
        to_z[i].start()
        src, dst = trios[i]
        dst[mine] = src[...]

    def pass_on(i):
        to_y[i].wait_recv()
        onward[i].start()

    def end_share(i):
        to_z[i].wait_recv()
        onward[i].wait_recv()

    order = (4, 3, 5, 2, 6, 1, 7)
    begin_share(0)
    for i in (1, 0, 2):
        for d in order:
            weight_copy(i, d).start()
        w3_ref[i, weight_rows] = weights[i][:, own_columns]
    begin_share(1)
    pass_on(0)
    end_share(0)

    def project(i):
        for d in order:
            weight_copy(i, d).wait_recv()
        return dot(fb_ref[...], w3_ref[i])

    def outward(i, k):
        axis, step = STEPS[k]
        return remote(own_ref.at[i], kv.at[k + 1, i], ksend.at[i, k + 1], krecv.at[i, k + 1], ring(axis, index[axis], step))

    def homeward(slot):
        pair = lax.div(slot - 1, 2)
        sign = 1 - 2 * lax.rem(slot - 1, 2)
        at_z = lax.div(pair, 2)
        at_y = pair - 2 * at_z
        at_x = 1 - at_y - at_z
        device = {
            "gx": lax.rem(index["gx"] - at_x * sign + 8, 8),
            "gy": lax.rem(index["gy"] - 2 * at_y * sign + 8, 8),
            "gz": lax.rem(index["gz"] - 2 * at_z * sign + 8, 8),
        }
        return remote(part.at[slot], back.at[slot], bsend.at[slot], brecv.at[slot], device)

    row_head = lax.broadcasted_iota(jnp.int32, (width, tokens), 0) // (width // 2)
    lane_head = lax.broadcasted_iota(jnp.int32, (tokens, width), 1) // (width // 2)

    def spread(value, turned, stacked):
        flipped = value.T
        for head in range(2):
            turned[:, head * tokens : (head + 1) * tokens] = jnp.where(row_head == head, flipped, 0.0).astype(BF16)
            stacked[head * tokens : (head + 1) * tokens, :] = jnp.where(lane_head == head, value, 0.0).astype(BF16)

    def send_own(i, w):
        value = project(w).astype(BF16)
        own_ref[i] = value
        kv[0, i] = value
        for k in (4, 5, 0, 1, 2, 3):
            outward(i, k).start()

    def reduce_x(m, d):
        target = lax.rem(x + d, 4)
        return remote(
            terms.at[target, pl.ds(2 * m, 2)], xr.at[d - 1, pl.ds(2 * m, 2)],
            xsend.at[d - 1, m], xrecv.at[d - 1, m], {"gy": 2 * target + y_bit},
        )

    def begin_term(m, term):
        split = term.reshape(8, 8, 8, width)
        for group in range(8):
            terms[group // 2, 2 * m + group % 2] = split[:, group].reshape(64, width).astype(BF16)
        for d in (2, 1, 3):
            reduce_x(m, d).start()

    send_own(0, 1)
    for zh in range(4):

        @pl.when(jnp.logical_and(out_from, 2 * zh + out_core != gz))
        def _():
            out_copy(zh).start()

    begin_share(2)
    send_own(1, 2)
    pass_on(1)
    spread(project(0).astype(BF16).astype(F32) * 0.125, qt, qs)
    top[...] = jnp.full_like(top, -jnp.inf)
    total[...] = jnp.zeros_like(total)
    dqt[...] = jnp.zeros_like(dqt)
    pass_on(2)
    ft[...] = fb_ref[...].astype(F32).T.astype(BF16)

    def arrived(i, slot):
        return remote(own_ref.at[i], kv.at[slot, i], ksend.at[i, slot], krecv.at[i, slot], ring("gx", index["gx"], 1))

    def first_pass(slot, unused):
        @pl.when(slot > 0)
        def _():
            arrived(0, slot).wait_recv()

        for c in range(4):
            columns = slice(c * chunk, (c + 1) * chunk)
            block = dot(kv[slot, 0], qt[:, columns])
            scores[slot, :, columns] = block
            old_top = top[:, columns]
            new_top = jnp.maximum(old_top, jnp.max(block, axis=0, keepdims=True))
            summed = jnp.sum(jnp.exp(block - new_top), axis=0, keepdims=True)
            total[:, columns] = total[:, columns] * jnp.exp(old_top - new_top) + summed
            top[:, columns] = new_top
        return unused

    lax.fori_loop(0, 7, first_pass, 0)
    top[...] = top[...] + jnp.log(total[...])
    for s in range(2):
        source = 4 * z_bit + 2 * y_bit + s

        @pl.when(source != gz)
        def _():
            remote(wo_ref, wob_ref.at[pl.ds(s * 64, 64)], osend.at[0], orecv.at[s], {"gz": source}).wait_recv()

        @pl.when(source == gz)
        def _():
            wob_ref[pl.ds(s * 64, 64)] = wo_ref[...]

    end_share(1)
    end_share(2)
    gown_ref[...] = gb_ref[:, own_columns]
    upstream = transpose_dot(gb_ref[...], wob_ref[...]).astype(BF16).astype(F32)
    spread(upstream, gt, gs)
    products = (upstream * ab_ref[:, own_columns].astype(F32)).T
    for head in range(2):
        rows = products[head * (width // 2) : (head + 1) * (width // 2)]
        delta_ref[:, head * tokens : (head + 1) * tokens] = jnp.sum(rows, axis=0, keepdims=True)

    at[...] = ab_ref[...].astype(F32).T.astype(BF16)
    begin_term(3, dot(at[...], gown_ref[...]))

    def second_pass(turn, unused):
        last = lax.div(turn, 6)
        group = lax.div(turn, 2)
        slot = (1 + 2 * lax.rem(group + 2, 3) + lax.rem(turn, 2)) * (1 - last)

        @pl.when(turn < 6)
        def _():
            arrived(1, slot).wait_recv()

        kt[...] = kv[slot, 0].astype(F32).T.astype(BF16)
        for c in range(4):
            columns = slice(c * chunk, (c + 1) * chunk)
            p = jnp.exp(scores[slot, :, columns] - top[:, columns]).astype(BF16)
            prob[:, columns] = p
            dp = dot(kv[slot, 1], gt[:, columns])
            ds = (p.astype(F32) * (dp - delta_ref[:, columns])).astype(BF16)
            grad[:, columns] = ds
            dqt[:, columns] += dot(kt[...], ds)
        part[slot, 0] = dot(grad[...], qs[...]).astype(BF16)
        part[slot, 1] = dot(prob[...], gs[...]).astype(BF16)

        @pl.when(turn < 6)
        def _():
            homeward(slot).start()

        return unused

    lax.fori_loop(0, 7, second_pass, 0)
    middle = width // 2
    turned = jnp.concatenate([dqt[:middle, :tokens], dqt[middle:, tokens:]], axis=0) * 0.125
    dq = turned.T.astype(BF16)
    begin_term(0, dot(ft[...], dq))
    across = transpose_dot(dq, w3_ref[0])
    for i in range(3):
        to_y[i].wait_send()
        to_z[i].wait_send()
        onward[i].wait_send()
        for d in order:
            weight_copy(i, d).wait_send()
    for zh in range(4):

        @pl.when(jnp.logical_and(out_from, 2 * zh + out_core != gz))
        def _():
            out_copy(zh).wait_send()

    for i in range(2):
        for k in range(6):
            outward(i, k).wait_send()
    for slot in (5, 6, 1, 2, 3, 4):
        homeward(slot).wait()
    for i in range(2):
        whole = part[0, i].astype(F32)
        for slot in range(1, 7):
            whole = whole + back[slot, i].astype(F32)
        pair_grad = whole.astype(BF16)
        begin_term(1 + i, dot(ft[...], pair_grad))
        across = across + transpose_dot(pair_grad, w3_ref[1 + i])
    partial_x[...] = across.astype(BF16)

    def join(copies):
        for copy in copies:
            copy.wait()

    def run(copies):
        for copy in copies:
            copy.start()

    owners = (
        (2 * (1 - y_bit) + 1 - z_bit, pair_both),
        (2 * (1 - y_bit) + z_bit, pair_y),
        (2 * y_bit + 1 - z_bit, pair_z),
    )
    g_copies = [
        remote(partial_x.at[slot_rows(slot)], gr.at[k], gsend.at[k], grecv.at[k], device)
        for k, (slot, device) in enumerate(owners)
    ]
    run(g_copies)
    for m in (3, 0, 1, 2):
        for d in (2, 1, 3):
            reduce_x(m, d).wait()
    whole = terms[x].astype(F32)
    for d in range(3):
        whole = whole + xr[d].astype(F32)
    s1[...] = whole.astype(BF16)
    y_copies = []
    for d in (4, 3, 5, 2, 6, 1, 7):
        target = lax.rem(gx + d, 8)
        y_copies.append(remote(s1.at[target], yr.at[d - 1], ysend.at[d - 1], yrecv.at[d - 1], {"gx": target}))
    run(y_copies)
    join(y_copies)
    whole = s1[gx].astype(F32)
    for d in range(7):
        whole = whole + yr[d].astype(F32)
    s2[...] = whole.reshape(8, 8, 128)
    z_copies = []
    for d in (4, 3, 5, 2, 6, 1, 7):
        target = lax.rem(gz + d, 8)
        z_copies.append(remote(s2.at[target], zr.at[gz], zsend.at[d - 1], zrecv.at[d - 1], {"gz": target}))
    run(z_copies)
    zr[gz] = s2[gz]
    join(z_copies)
    lower = zr[0] + zr[2] + zr[4] + zr[6]
    upper = zr[1] + zr[3] + zr[5] + zr[7]
    u[gx] = jnp.concatenate([lower, upper], axis=0).astype(BF16)
    u_copies = []
    for d in (4, 3, 5, 2, 6, 1, 7):
        u_copies.append(remote(u.at[gx], u.at[gx], usend.at[d - 1], urecv.at[d - 1], ring("gx", gx, d)))
    run(u_copies)
    join(g_copies)
    whole = partial_x[mine].astype(F32)
    for k in range(3):
        whole = whole + gr[k].astype(F32)
    gx_ref[...] = whole.astype(BF16)
    join(u_copies)
    h_copies = []
    for d in (4, 3, 5, 2, 6, 1, 7):
        h_copies.append(remote(u, h_ref.at[gy], hsend.at[d - 1], hrecv.at[d - 1], ring("gy", gy, d)))
    run(h_copies)
    h_ref[gy] = u[...]
    join(h_copies)


def finish_kernel(h_ref, g_ref, gx_ref, *out_refs):
    for gy in range(8):
        for gx in range(8):
            x, y_bit, m, r = gy // 2, gy % 2, gx // 2, gx % 2
            tile = h_ref[gy, gx].astype(F32)
            for z_bit in range(2):
                column = (2 * z_bit + y_bit) * 128
                out_refs[m][16 * x + 8 * r : 16 * x + 8 * r + 8, column : column + 128] = tile[8 * z_bit : 8 * z_bit + 8]
    for i in range(gx_ref.shape[0]):
        rows = g_ref[16 * i : 16 * i + 16].astype(F32)
        for j in range(4):
            gx_ref[i, j] = rows[4 * j : 4 * j + 4].astype(BF16)


def vmem(count):
    return [pl.BlockSpec(memory_space=pltpu.VMEM)] * count


def dma(*shape):
    return pltpu.SemaphoreType.DMA(shape)


def call(kernel, number, shapes, scratch, *operands):
    return pl.pallas_call(
        kernel,
        out_shape=[jax.ShapeDtypeStruct(shape, BF16) for shape in shapes],
        in_specs=vmem(len(operands)),
        out_specs=vmem(len(shapes)),
        scratch_shapes=scratch,
        compiler_params=pltpu.CompilerParams(collective_id=number, has_side_effects=True),
    )(*operands)


def transpose_dot(left, right):
    return lax.dot_general(left, right, (((1,), (1,)), ((), ())), preferred_element_type=F32)


def dot(left, right):
    return jnp.dot(left, right, preferred_element_type=F32)


def on_device(features, grad_y, attn_out, w_query, w_key, w_value, w_out):
    width = features.shape[3]
    local = features.shape[0] * features.shape[1] * features.shape[2]
    tokens = 4 * local
    quarter = width // 4
    rows, grad_x = call(
        block_kernel,
        0,
        [(8, 8, 16, quarter), (local, width)],
        [
            pltpu.VMEM((local, width), BF16),
            pltpu.VMEM((local, width), BF16),
            pltpu.VMEM((local, width), BF16),
            pltpu.VMEM((local, width), F32),
            pltpu.VMEM((tokens, width), BF16),
            pltpu.VMEM((tokens, width), BF16),
            pltpu.VMEM((tokens, quarter), BF16),
            pltpu.VMEM((3, width, quarter), BF16),
            pltpu.VMEM((width, tokens), BF16),
            pltpu.VMEM((width, tokens), BF16),
            pltpu.VMEM((tokens, width), BF16),
            pltpu.VMEM((quarter, width), BF16),
            pltpu.VMEM((2, tokens, quarter), BF16),
            pltpu.VMEM((1, 2 * tokens), F32),
            pltpu.VMEM((7, 2, tokens, quarter), BF16),
            pltpu.VMEM((7, tokens, 2 * tokens), F32),
            pltpu.VMEM((7, 2, tokens, quarter), BF16),
            pltpu.VMEM((7, 2, tokens, quarter), BF16),
            pltpu.VMEM((quarter, 2 * tokens), BF16),
            pltpu.VMEM((quarter, 2 * tokens), BF16),
            pltpu.VMEM((quarter, tokens), BF16),
            pltpu.VMEM((2 * tokens, quarter), BF16),
            pltpu.VMEM((2 * tokens, quarter), BF16),
            pltpu.VMEM((tokens, 2 * tokens), BF16),
            pltpu.VMEM((tokens, 2 * tokens), BF16),
            pltpu.VMEM((quarter, 2 * tokens), F32),
            pltpu.VMEM((1, 2 * tokens), F32),
            pltpu.VMEM((1, 2 * tokens), F32),
            pltpu.VMEM((4, 8, 64, quarter), BF16),
            pltpu.VMEM((tokens, width), BF16),
            pltpu.VMEM((3, 8, 64, quarter), BF16),
            pltpu.VMEM((8, 64, quarter), BF16),
            pltpu.VMEM((7, 64, quarter), BF16),
            pltpu.VMEM((8, 8, quarter), F32),
            pltpu.VMEM((8, 8, quarter), F32),
            pltpu.VMEM((8, 16, quarter), BF16),
            pltpu.VMEM((3, local, width), BF16),
            dma(3, 3), dma(3, 3), dma(7, 3), dma(7, 3), dma(4), dma(2),
            dma(2, 7), dma(2, 7), dma(7), dma(7),
            dma(3, 4), dma(3, 4), dma(7), dma(7), dma(7), dma(7), dma(7), dma(7), dma(7), dma(7), dma(3), dma(3),
        ],
        features, grad_y, attn_out, w_query, w_key, w_value, w_out,
    )
    outs = pl.pallas_call(
        finish_kernel,
        out_shape=[jax.ShapeDtypeStruct(features.shape, BF16)] + [jax.ShapeDtypeStruct((64, width), F32)] * 4,
        in_specs=vmem(2),
        out_specs=vmem(5),
    )(rows, grad_x)
    return tuple(outs)


def solution(mesh):
    token_spec = P("gx", "gy", "gz", None)
    row_spec = P("gz", None)
    return jax.shard_map(
        on_device,
        mesh=mesh,
        in_specs=(token_spec,) * 3 + (row_spec,) * 4,
        out_specs=(token_spec,) + (row_spec,) * 4,
        check_vma=False,
    )
```

```python
import jax
import jax.numpy as jnp
from jax import lax
from jax.experimental import pallas as pl
from jax.experimental.pallas import tpu as pltpu
from jax.sharding import PartitionSpec as P

HEADS = 8
MESH = pl.DeviceIdType.MESH
STEPS = (("gx", 1), ("gx", -1), ("gy", 2), ("gy", -2), ("gz", 2), ("gz", -2))
BF16 = jnp.bfloat16
F32 = jnp.float32


def remote(src, dst, send, recv, device):
    return pltpu.make_async_remote_copy(
        src_ref=src, dst_ref=dst, send_sem=send, recv_sem=recv, device_id=device, device_id_type=MESH
    )


def greet(devices):
    barrier = pltpu.get_barrier_semaphore()
    for device in devices:
        pl.semaphore_signal(barrier, inc=1, device_id=device, device_id_type=MESH)
    pl.semaphore_wait(barrier, len(devices))


def ring(axis, index, step):
    return {axis: lax.rem(index + step + 8, 8)}


def block_kernel(
    f_in, g_in, a_in, wq_ref, wk_ref, wv_ref, wo_ref,
    h_ref, gx_ref,
    f_ref, g_ref, a_ref, stage,
    fb_ref, ab_ref, gown_ref, w3_ref, ft, at,
    gb_ref, wob_ref, own_ref, delta_ref,
    kv, scores, part, back, qt, gt, kt, qs, gs, prob, grad, dqt, top, total,
    terms, partial_x, xr, s1, yr, s2, zr, u, gr,
    rsend, rrecv, wsend, wrecv, osend, orecv, vsend, vrecv,
    ksend, krecv, bsend, brecv,
    xsend, xrecv, ysend, yrecv, zsend, zrecv, usend, urecv, hsend, hrecv, gsend, grecv,
):
    index = {axis: lax.axis_index(axis) for axis in ("gx", "gy", "gz")}
    gx, gy, gz = index["gx"], index["gy"], index["gz"]
    tokens, width = gown_ref.shape
    local = f_ref.shape[0]
    chunk = tokens // 2
    y_bit, z_bit = lax.rem(gy, 2), lax.rem(gz, 2)
    pair_z = {"gz": gz + 1 - 2 * z_bit}
    pair_y = {"gy": gy + 1 - 2 * y_bit}
    own_columns = pl.ds(pl.multiple_of(z_bit * 256 + y_bit * 128, 128), 128)
    pair_both = {"gy": pair_y["gy"], "gz": pair_z["gz"]}
    x = lax.div(gy, 2)
    greet([ring(axis, index[axis], d) for axis in ("gx", "gy", "gz") for d in range(1, 8)] + [pair_both])

    def slot_rows(slot):
        return pl.ds(pl.multiple_of(slot * local, local), local)

    mine = slot_rows(2 * y_bit + z_bit)
    theirs = slot_rows(2 * (1 - y_bit) + z_bit)

    def flatten(source, target):
        for i in range(source.shape[0]):
            for j in range(4):
                stage[16 * i + 4 * j : 16 * i + 4 * j + 4] = source[i, j].astype(F32)
        target[...] = stage[...].astype(BF16)

    trios = ((f_ref, fb_ref), (g_ref, gb_ref), (a_ref, ab_ref))
    to_y = [remote(src, dst.at[mine], rsend.at[0, i], rrecv.at[0, i], pair_y) for i, (src, dst) in enumerate(trios)]
    to_z = [remote(src, dst.at[mine], rsend.at[1, i], rrecv.at[1, i], pair_z) for i, (src, dst) in enumerate(trios)]
    onward = [
        remote(dst.at[theirs], dst.at[theirs], rsend.at[2, i], rrecv.at[2, i], pair_z)
        for i, (src, dst) in enumerate(trios)
    ]
    weights = (wq_ref, wk_ref, wv_ref)
    x_rows = pl.ds(pl.multiple_of(x * 16, 16), 16)

    def x_peer(d):
        return {"gy": 2 * lax.rem(x + d, 4) + y_bit}

    def weight_share(i, d):
        return remote(w3_ref.at[i, :, x], w3_ref.at[i, :, x], vsend.at[d - 1, i], vrecv.at[d - 1, i], x_peer(d))

    def out_share(d):
        return remote(wob_ref.at[:, x], wob_ref.at[:, x], vsend.at[d - 1, 3], vrecv.at[d - 1, 3], x_peer(d))

    def weight_copy(i, d):
        target = lax.rem(gz + d, 8)
        columns = pl.ds(pl.multiple_of(lax.rem(target, 2) * 256 + y_bit * 128, 128), 128)
        return remote(
            weights[i].at[x_rows, columns], w3_ref.at[i, gz, x], wsend.at[d - 1, i], wrecv.at[d - 1, i], {"gz": target}
        )

    half = lax.rem(gz, 2)
    out_core = lax.div(gz, 4)
    out_from = lax.rem(lax.div(gz, 2), 2) == y_bit

    def out_copy(zh):
        return remote(wo_ref.at[x_rows], wob_ref.at[half, x], osend.at[zh], orecv.at[half], {"gz": 2 * zh + out_core})

    def begin_share(i):
        flatten((f_in, g_in, a_in)[i], trios[i][0])
        to_y[i].start()
        to_z[i].start()
        src, dst = trios[i]
        dst[mine] = src[...]

    def pass_on(i):
        to_y[i].wait_recv()
        onward[i].start()

    def end_share(i):
        to_z[i].wait_recv()
        onward[i].wait_recv()

    order = (4, 3, 5, 2, 6, 1, 7)
    begin_share(0)
    for i in (1, 0, 2):
        for d in order:
            weight_copy(i, d).start()
        w3_ref[i, gz, x] = weights[i][x_rows, own_columns]
    for zh in range(4):

        @pl.when(jnp.logical_and(out_from, 2 * zh + out_core != gz))
        def _():
            out_copy(zh).start()

    begin_share(1)
    pass_on(0)
    for i in (1, 0, 2):
        for d in order:
            weight_copy(i, d).wait_recv()
        for d in (2, 1, 3):
            weight_share(i, d).start()
    for s in range(2):
        source = 4 * z_bit + 2 * y_bit + s

        @pl.when(source != gz)
        def _():
            remote(wo_ref.at[x_rows], wob_ref.at[s, x], osend.at[0], orecv.at[s], {"gz": source}).wait_recv()

        @pl.when(source == gz)
        def _():
            wob_ref[s, x] = wo_ref[x_rows]

    for d in (2, 1, 3):
        out_share(d).start()
    end_share(0)

    def project(i):
        for d in (2, 1, 3):
            weight_share(i, d).wait_recv()
        return dot(fb_ref[...], w3_ref[i].reshape(tokens, width))

    def outward(i, k):
        axis, step = STEPS[k]
        return remote(own_ref.at[i], kv.at[k + 1, i], ksend.at[i, k + 1], krecv.at[i, k + 1], ring(axis, index[axis], step))

    def homeward(slot):
        pair = lax.div(slot - 1, 2)
        sign = 1 - 2 * lax.rem(slot - 1, 2)
        at_z = lax.div(pair, 2)
        at_y = pair - 2 * at_z
        at_x = 1 - at_y - at_z
        device = {
            "gx": lax.rem(index["gx"] - at_x * sign + 8, 8),
            "gy": lax.rem(index["gy"] - 2 * at_y * sign + 8, 8),
            "gz": lax.rem(index["gz"] - 2 * at_z * sign + 8, 8),
        }
        return remote(part.at[slot], back.at[slot], bsend.at[slot], brecv.at[slot], device)

    row_head = lax.broadcasted_iota(jnp.int32, (width, tokens), 0) // (width // 2)
    lane_head = lax.broadcasted_iota(jnp.int32, (tokens, width), 1) // (width // 2)

    def spread(value, turned, stacked):
        flipped = value.T
        for head in range(2):
            turned[:, head * tokens : (head + 1) * tokens] = jnp.where(row_head == head, flipped, 0.0).astype(BF16)
            stacked[head * tokens : (head + 1) * tokens, :] = jnp.where(lane_head == head, value, 0.0).astype(BF16)

    def send_own(i, w):
        value = project(w).astype(BF16)
        own_ref[i] = value
        kv[0, i] = value
        for k in (4, 5, 0, 1, 2, 3):
            outward(i, k).start()

    def reduce_x(m, d):
        target = lax.rem(x + d, 4)
        return remote(
            terms.at[target, pl.ds(2 * m, 2)], xr.at[d - 1, pl.ds(2 * m, 2)],
            xsend.at[d - 1, m], xrecv.at[d - 1, m], {"gy": 2 * target + y_bit},
        )

    def begin_term(m, term):
        split = term.reshape(8, 8, 8, width)
        for group in range(8):
            terms[group // 2, 2 * m + group % 2] = split[:, group].reshape(64, width).astype(BF16)
        for d in (2, 1, 3):
            reduce_x(m, d).start()

    send_own(0, 1)
    begin_share(2)
    send_own(1, 2)
    pass_on(1)
    spread(project(0).astype(BF16).astype(F32) * 0.125, qt, qs)
    top[...] = jnp.full_like(top, -jnp.inf)
    total[...] = jnp.zeros_like(total)
    dqt[...] = jnp.zeros_like(dqt)
    pass_on(2)
    ft[...] = fb_ref[...].astype(F32).T.astype(BF16)

    def arrived(i, slot):
        return remote(own_ref.at[i], kv.at[slot, i], ksend.at[i, slot], krecv.at[i, slot], ring("gx", index["gx"], 1))

    def first_pass(slot, unused):
        @pl.when(slot > 0)
        def _():
            arrived(0, slot).wait_recv()

        for c in range(4):
            columns = slice(c * chunk, (c + 1) * chunk)
            block = dot(kv[slot, 0], qt[:, columns])
            scores[slot, :, columns] = block
            old_top = top[:, columns]
            new_top = jnp.maximum(old_top, jnp.max(block, axis=0, keepdims=True))
            summed = jnp.sum(jnp.exp(block - new_top), axis=0, keepdims=True)
            total[:, columns] = total[:, columns] * jnp.exp(old_top - new_top) + summed
            top[:, columns] = new_top
        return unused

    lax.fori_loop(0, 7, first_pass, 0)
    top[...] = top[...] + jnp.log(total[...])
    for d in (2, 1, 3):
        out_share(d).wait_recv()
    end_share(1)
    end_share(2)
    gown_ref[...] = gb_ref[:, own_columns]
    upstream = transpose_dot(gb_ref[...], wob_ref[...].reshape(width, gb_ref.shape[1])).astype(BF16).astype(F32)
    spread(upstream, gt, gs)
    products = (upstream * ab_ref[:, own_columns].astype(F32)).T
    for head in range(2):
        rows = products[head * (width // 2) : (head + 1) * (width // 2)]
        delta_ref[:, head * tokens : (head + 1) * tokens] = jnp.sum(rows, axis=0, keepdims=True)

    at[...] = ab_ref[...].astype(F32).T.astype(BF16)
    begin_term(3, dot(at[...], gown_ref[...]))

    def second_pass(turn, unused):
        last = lax.div(turn, 6)
        group = lax.div(turn, 2)
        slot = (1 + 2 * lax.rem(group + 2, 3) + lax.rem(turn, 2)) * (1 - last)

        @pl.when(turn < 6)
        def _():
            arrived(1, slot).wait_recv()

        kt[...] = kv[slot, 0].astype(F32).T.astype(BF16)
        for c in range(4):
            columns = slice(c * chunk, (c + 1) * chunk)
            p = jnp.exp(scores[slot, :, columns] - top[:, columns]).astype(BF16)
            prob[:, columns] = p
            dp = dot(kv[slot, 1], gt[:, columns])
            ds = (p.astype(F32) * (dp - delta_ref[:, columns])).astype(BF16)
            grad[:, columns] = ds
            dqt[:, columns] += dot(kt[...], ds)
        part[slot, 0] = dot(grad[...], qs[...]).astype(BF16)
        part[slot, 1] = dot(prob[...], gs[...]).astype(BF16)

        @pl.when(turn < 6)
        def _():
            homeward(slot).start()

        return unused

    lax.fori_loop(0, 7, second_pass, 0)
    middle = width // 2
    turned = jnp.concatenate([dqt[:middle, :tokens], dqt[middle:, tokens:]], axis=0) * 0.125
    dq = turned.T.astype(BF16)
    begin_term(0, dot(ft[...], dq))
    across = transpose_dot(dq, w3_ref[0].reshape(tokens, width))
    for i in range(3):
        to_y[i].wait_send()
        to_z[i].wait_send()
        onward[i].wait_send()
        for d in order:
            weight_copy(i, d).wait_send()
        for d in (2, 1, 3):
            weight_share(i, d).wait_send()
    for d in (2, 1, 3):
        out_share(d).wait_send()
    for zh in range(4):

        @pl.when(jnp.logical_and(out_from, 2 * zh + out_core != gz))
        def _():
            out_copy(zh).wait_send()

    for i in range(2):
        for k in range(6):
            outward(i, k).wait_send()
    for slot in (5, 6, 1, 2, 3, 4):
        homeward(slot).wait()
    for i in range(2):
        whole = part[0, i].astype(F32)
        for slot in range(1, 7):
            whole = whole + back[slot, i].astype(F32)
        pair_grad = whole.astype(BF16)
        begin_term(1 + i, dot(ft[...], pair_grad))
        across = across + transpose_dot(pair_grad, w3_ref[1 + i].reshape(tokens, width))
    partial_x[...] = across.astype(BF16)

    def join(copies):
        for copy in copies:
            copy.wait()

    def run(copies):
        for copy in copies:
            copy.start()

    owners = (
        (2 * (1 - y_bit) + 1 - z_bit, pair_both),
        (2 * (1 - y_bit) + z_bit, pair_y),
        (2 * y_bit + 1 - z_bit, pair_z),
    )
    g_copies = [
        remote(partial_x.at[slot_rows(slot)], gr.at[k], gsend.at[k], grecv.at[k], device)
        for k, (slot, device) in enumerate(owners)
    ]
    run(g_copies)
    for m in (3, 0, 1, 2):
        for d in (2, 1, 3):
            reduce_x(m, d).wait()
    whole = terms[x].astype(F32)
    for d in range(3):
        whole = whole + xr[d].astype(F32)
    s1[...] = whole.astype(BF16)
    y_copies = []
    for d in (4, 3, 5, 2, 6, 1, 7):
        target = lax.rem(gx + d, 8)
        y_copies.append(remote(s1.at[target], yr.at[d - 1], ysend.at[d - 1], yrecv.at[d - 1], {"gx": target}))
    run(y_copies)
    join(y_copies)
    whole = s1[gx].astype(F32)
    for d in range(7):
        whole = whole + yr[d].astype(F32)
    s2[...] = whole.reshape(8, 8, 128)
    z_copies = []
    for d in (4, 3, 5, 2, 6, 1, 7):
        target = lax.rem(gz + d, 8)
        z_copies.append(remote(s2.at[target], zr.at[gz], zsend.at[d - 1], zrecv.at[d - 1], {"gz": target}))
    run(z_copies)
    zr[gz] = s2[gz]
    join(z_copies)
    lower = zr[0] + zr[2] + zr[4] + zr[6]
    upper = zr[1] + zr[3] + zr[5] + zr[7]
    u[gx] = jnp.concatenate([lower, upper], axis=0).astype(BF16)
    u_copies = []
    for d in (4, 3, 5, 2, 6, 1, 7):
        u_copies.append(remote(u.at[gx], u.at[gx], usend.at[d - 1], urecv.at[d - 1], ring("gx", gx, d)))
    run(u_copies)
    join(g_copies)
    whole = partial_x[mine].astype(F32)
    for k in range(3):
        whole = whole + gr[k].astype(F32)
    gx_ref[...] = whole.astype(BF16)
    join(u_copies)
    h_copies = []
    for d in (4, 3, 5, 2, 6, 1, 7):
        h_copies.append(remote(u, h_ref.at[gy], hsend.at[d - 1], hrecv.at[d - 1], ring("gy", gy, d)))
    run(h_copies)
    h_ref[gy] = u[...]
    join(h_copies)


def finish_kernel(h_ref, g_ref, gx_ref, *out_refs):
    for gy in range(8):
        for gx in range(8):
            x, y_bit, m, r = gy // 2, gy % 2, gx // 2, gx % 2
            tile = h_ref[gy, gx].astype(F32)
            for z_bit in range(2):
                column = (2 * z_bit + y_bit) * 128
                out_refs[m][16 * x + 8 * r : 16 * x + 8 * r + 8, column : column + 128] = tile[8 * z_bit : 8 * z_bit + 8]
    for i in range(gx_ref.shape[0]):
        rows = g_ref[16 * i : 16 * i + 16].astype(F32)
        for j in range(4):
            gx_ref[i, j] = rows[4 * j : 4 * j + 4].astype(BF16)


def vmem(count):
    return [pl.BlockSpec(memory_space=pltpu.VMEM)] * count


def dma(*shape):
    return pltpu.SemaphoreType.DMA(shape)


def call(kernel, number, shapes, scratch, *operands):
    return pl.pallas_call(
        kernel,
        out_shape=[jax.ShapeDtypeStruct(shape, BF16) for shape in shapes],
        in_specs=vmem(len(operands)),
        out_specs=vmem(len(shapes)),
        scratch_shapes=scratch,
        compiler_params=pltpu.CompilerParams(collective_id=number, has_side_effects=True),
    )(*operands)


def transpose_dot(left, right):
    return lax.dot_general(left, right, (((1,), (1,)), ((), ())), preferred_element_type=F32)


def dot(left, right):
    return jnp.dot(left, right, preferred_element_type=F32)


def on_device(features, grad_y, attn_out, w_query, w_key, w_value, w_out):
    width = features.shape[3]
    local = features.shape[0] * features.shape[1] * features.shape[2]
    tokens = 4 * local
    quarter = width // 4
    rows, grad_x = call(
        block_kernel,
        0,
        [(8, 8, 16, quarter), (local, width)],
        [
            pltpu.VMEM((local, width), BF16),
            pltpu.VMEM((local, width), BF16),
            pltpu.VMEM((local, width), BF16),
            pltpu.VMEM((local, width), F32),
            pltpu.VMEM((tokens, width), BF16),
            pltpu.VMEM((tokens, width), BF16),
            pltpu.VMEM((tokens, quarter), BF16),
            pltpu.VMEM((3, 8, 4, 16, quarter), BF16),
            pltpu.VMEM((width, tokens), BF16),
            pltpu.VMEM((width, tokens), BF16),
            pltpu.VMEM((tokens, width), BF16),
            pltpu.VMEM((2, 4, 16, width), BF16),
            pltpu.VMEM((2, tokens, quarter), BF16),
            pltpu.VMEM((1, 2 * tokens), F32),
            pltpu.VMEM((7, 2, tokens, quarter), BF16),
            pltpu.VMEM((7, tokens, 2 * tokens), F32),
            pltpu.VMEM((7, 2, tokens, quarter), BF16),
            pltpu.VMEM((7, 2, tokens, quarter), BF16),
            pltpu.VMEM((quarter, 2 * tokens), BF16),
            pltpu.VMEM((quarter, 2 * tokens), BF16),
            pltpu.VMEM((quarter, tokens), BF16),
            pltpu.VMEM((2 * tokens, quarter), BF16),
            pltpu.VMEM((2 * tokens, quarter), BF16),
            pltpu.VMEM((tokens, 2 * tokens), BF16),
            pltpu.VMEM((tokens, 2 * tokens), BF16),
            pltpu.VMEM((quarter, 2 * tokens), F32),
            pltpu.VMEM((1, 2 * tokens), F32),
            pltpu.VMEM((1, 2 * tokens), F32),
            pltpu.VMEM((4, 8, 64, quarter), BF16),
            pltpu.VMEM((tokens, width), BF16),
            pltpu.VMEM((3, 8, 64, quarter), BF16),
            pltpu.VMEM((8, 64, quarter), BF16),
            pltpu.VMEM((7, 64, quarter), BF16),
            pltpu.VMEM((8, 8, quarter), F32),
            pltpu.VMEM((8, 8, quarter), F32),
            pltpu.VMEM((8, 16, quarter), BF16),
            pltpu.VMEM((3, local, width), BF16),
            dma(3, 3), dma(3, 3), dma(7, 3), dma(7, 3), dma(4), dma(2), dma(3, 4), dma(3, 4),
            dma(2, 7), dma(2, 7), dma(7), dma(7),
            dma(3, 4), dma(3, 4), dma(7), dma(7), dma(7), dma(7), dma(7), dma(7), dma(7), dma(7), dma(3), dma(3),
        ],
        features, grad_y, attn_out, w_query, w_key, w_value, w_out,
    )
    outs = pl.pallas_call(
        finish_kernel,
        out_shape=[jax.ShapeDtypeStruct(features.shape, BF16)] + [jax.ShapeDtypeStruct((64, width), F32)] * 4,
        in_specs=vmem(2),
        out_specs=vmem(5),
    )(rows, grad_x)
    return tuple(outs)


def solution(mesh):
    token_spec = P("gx", "gy", "gz", None)
    row_spec = P("gz", None)
    return jax.shard_map(
        on_device,
        mesh=mesh,
        in_specs=(token_spec,) * 3 + (row_spec,) * 4,
        out_specs=(token_spec,) + (row_spec,) * 4,
        check_vma=False,
    )
```

```python
import jax
import jax.numpy as jnp
from jax import lax
from jax.experimental import pallas as pl
from jax.experimental.pallas import tpu as pltpu
from jax.sharding import PartitionSpec as P

HEADS = 8
MESH = pl.DeviceIdType.MESH
STEPS = (("gx", 1), ("gx", -1), ("gy", 2), ("gy", -2), ("gz", 2), ("gz", -2))
BF16 = jnp.bfloat16
F32 = jnp.float32


def remote(src, dst, send, recv, device):
    return pltpu.make_async_remote_copy(
        src_ref=src, dst_ref=dst, send_sem=send, recv_sem=recv, device_id=device, device_id_type=MESH
    )


def greet(devices, meanwhile):
    barrier = pltpu.get_barrier_semaphore()
    for device in devices:
        pl.semaphore_signal(barrier, inc=1, device_id=device, device_id_type=MESH)
    meanwhile()
    pl.semaphore_wait(barrier, len(devices))


def ring(axis, index, step):
    return {axis: lax.rem(index + step + 8, 8)}


def block_kernel(
    f_in, g_in, a_in, wq_ref, wk_ref, wv_ref, wo_ref,
    h_ref, gx_ref,
    f_ref, g_ref, a_ref, stage,
    fb_ref, ab_ref, gown_ref, w3_ref, ft, at,
    gb_ref, wob_ref, own_ref, delta_ref,
    kv, scores, part, back, qt, gt, kt, qs, gs, prob, grad, dqt, top, total,
    terms, partial_x, xr, s1, yr, s2, zr, u, gr,
    rsend, rrecv, wsend, wrecv, osend, orecv, vsend, vrecv,
    ksend, krecv, bsend, brecv,
    xsend, xrecv, ysend, yrecv, zsend, zrecv, usend, urecv, hsend, hrecv, gsend, grecv,
):
    index = {axis: lax.axis_index(axis) for axis in ("gx", "gy", "gz")}
    gx, gy, gz = index["gx"], index["gy"], index["gz"]
    tokens, width = gown_ref.shape
    local = f_ref.shape[0]
    chunk = tokens // 2
    y_bit, z_bit = lax.rem(gy, 2), lax.rem(gz, 2)
    pair_z = {"gz": gz + 1 - 2 * z_bit}
    pair_y = {"gy": gy + 1 - 2 * y_bit}
    own_columns = pl.ds(pl.multiple_of(z_bit * 256 + y_bit * 128, 128), 128)
    pair_both = {"gy": pair_y["gy"], "gz": pair_z["gz"]}
    x = lax.div(gy, 2)
    def flatten(source, target):
        for i in range(source.shape[0]):
            for j in range(4):
                stage[16 * i + 4 * j : 16 * i + 4 * j + 4] = source[i, j].astype(F32)
        target[...] = stage[...].astype(BF16)

    greet([ring(axis, index[axis], d) for axis in ("gx", "gy", "gz") for d in range(1, 8)] + [pair_both], lambda: flatten(f_in, f_ref))

    def slot_rows(slot):
        return pl.ds(pl.multiple_of(slot * local, local), local)

    mine = slot_rows(2 * y_bit + z_bit)
    theirs = slot_rows(2 * (1 - y_bit) + z_bit)

    trios = ((f_ref, fb_ref), (g_ref, gb_ref), (a_ref, ab_ref))
    to_y = [remote(src, dst.at[mine], rsend.at[0, i], rrecv.at[0, i], pair_y) for i, (src, dst) in enumerate(trios)]
    to_z = [remote(src, dst.at[mine], rsend.at[1, i], rrecv.at[1, i], pair_z) for i, (src, dst) in enumerate(trios)]
    onward = [
        remote(dst.at[theirs], dst.at[theirs], rsend.at[2, i], rrecv.at[2, i], pair_z)
        for i, (src, dst) in enumerate(trios)
    ]
    weights = (wq_ref, wk_ref, wv_ref)
    x_rows = pl.ds(pl.multiple_of(x * 16, 16), 16)

    def x_peer(d):
        return {"gy": 2 * lax.rem(x + d, 4) + y_bit}

    def weight_share(i, d):
        return remote(w3_ref.at[i, :, x], w3_ref.at[i, :, x], vsend.at[d - 1, i], vrecv.at[d - 1, i], x_peer(d))

    def out_share(d):
        return remote(wob_ref.at[:, x], wob_ref.at[:, x], vsend.at[d - 1, 3], vrecv.at[d - 1, 3], x_peer(d))

    def weight_copy(i, d):
        target = lax.rem(gz + d, 8)
        columns = pl.ds(pl.multiple_of(lax.rem(target, 2) * 256 + y_bit * 128, 128), 128)
        return remote(
            weights[i].at[x_rows, columns], w3_ref.at[i, gz, x], wsend.at[d - 1, i], wrecv.at[d - 1, i], {"gz": target}
        )

    half = lax.rem(gz, 2)
    out_core = lax.div(gz, 4)
    out_from = lax.rem(lax.div(gz, 2), 2) == y_bit

    def out_copy(zh):
        return remote(wo_ref.at[x_rows], wob_ref.at[half, x], osend.at[zh], orecv.at[half], {"gz": 2 * zh + out_core})

    def begin_share(i):
        if i > 0:
            flatten((f_in, g_in, a_in)[i], trios[i][0])
        to_y[i].start()
        to_z[i].start()
        src, dst = trios[i]
        dst[mine] = src[...]

    def pass_on(i):
        to_y[i].wait_recv()
        onward[i].start()

    def end_share(i):
        to_z[i].wait_recv()
        onward[i].wait_recv()

    order = (4, 3, 5, 2, 6, 1, 7)
    begin_share(0)
    for i in (1, 0, 2):
        for d in order:
            weight_copy(i, d).start()
        w3_ref[i, gz, x] = weights[i][x_rows, own_columns]
    for zh in range(4):

        @pl.when(jnp.logical_and(out_from, 2 * zh + out_core != gz))
        def _():
            out_copy(zh).start()

    begin_share(1)
    pass_on(0)
    for i in (1, 0, 2):
        for d in order:
            weight_copy(i, d).wait_recv()
        for d in (2, 1, 3):
            weight_share(i, d).start()
    for s in range(2):
        source = 4 * z_bit + 2 * y_bit + s

        @pl.when(source != gz)
        def _():
            remote(wo_ref.at[x_rows], wob_ref.at[s, x], osend.at[0], orecv.at[s], {"gz": source}).wait_recv()

        @pl.when(source == gz)
        def _():
            wob_ref[s, x] = wo_ref[x_rows]

    for d in (2, 1, 3):
        out_share(d).start()
    end_share(0)

    def project(i):
        for d in (2, 1, 3):
            weight_share(i, d).wait_recv()
        return dot(fb_ref[...], w3_ref[i].reshape(tokens, width))

    def outward(i, k):
        axis, step = STEPS[k]
        return remote(own_ref.at[i], kv.at[k + 1, i], ksend.at[i, k + 1], krecv.at[i, k + 1], ring(axis, index[axis], step))

    def homeward(slot):
        pair = lax.div(slot - 1, 2)
        sign = 1 - 2 * lax.rem(slot - 1, 2)
        at_z = lax.div(pair, 2)
        at_y = pair - 2 * at_z
        at_x = 1 - at_y - at_z
        device = {
            "gx": lax.rem(index["gx"] - at_x * sign + 8, 8),
            "gy": lax.rem(index["gy"] - 2 * at_y * sign + 8, 8),
            "gz": lax.rem(index["gz"] - 2 * at_z * sign + 8, 8),
        }
        return remote(part.at[slot], back.at[slot], bsend.at[slot], brecv.at[slot], device)

    row_head = lax.broadcasted_iota(jnp.int32, (width, tokens), 0) // (width // 2)
    lane_head = lax.broadcasted_iota(jnp.int32, (tokens, width), 1) // (width // 2)

    def spread(value, turned, stacked):
        flipped = value.T
        for head in range(2):
            turned[:, head * tokens : (head + 1) * tokens] = jnp.where(row_head == head, flipped, 0.0).astype(BF16)
            stacked[head * tokens : (head + 1) * tokens, :] = jnp.where(lane_head == head, value, 0.0).astype(BF16)

    def send_own(i, w):
        value = project(w).astype(BF16)
        own_ref[i] = value
        kv[0, i] = value
        for k in (4, 5, 0, 1, 2, 3):
            outward(i, k).start()

    def reduce_x(m, d):
        target = lax.rem(x + d, 4)
        return remote(
            terms.at[target, pl.ds(2 * m, 2)], xr.at[d - 1, pl.ds(2 * m, 2)],
            xsend.at[d - 1, m], xrecv.at[d - 1, m], {"gy": 2 * target + y_bit},
        )

    def begin_term(m, term):
        split = term.reshape(8, 8, 8, width)
        for group in range(8):
            terms[group // 2, 2 * m + group % 2] = split[:, group].reshape(64, width).astype(BF16)
        for d in (2, 1, 3):
            reduce_x(m, d).start()

    send_own(0, 1)
    begin_share(2)
    send_own(1, 2)
    pass_on(1)
    spread(project(0).astype(BF16).astype(F32) * 0.125, qt, qs)
    top[...] = jnp.full_like(top, -jnp.inf)
    total[...] = jnp.zeros_like(total)
    dqt[...] = jnp.zeros_like(dqt)
    pass_on(2)
    ft[...] = fb_ref[...].astype(F32).T.astype(BF16)

    def arrived(i, slot):
        return remote(own_ref.at[i], kv.at[slot, i], ksend.at[i, slot], krecv.at[i, slot], ring("gx", index["gx"], 1))

    def first_pass(slot, unused):
        @pl.when(slot > 0)
        def _():
            arrived(0, slot).wait_recv()

        for c in range(4):
            columns = slice(c * chunk, (c + 1) * chunk)
            block = dot(kv[slot, 0], qt[:, columns])
            scores[slot, :, columns] = block
            old_top = top[:, columns]
            new_top = jnp.maximum(old_top, jnp.max(block, axis=0, keepdims=True))
            summed = jnp.sum(jnp.exp(block - new_top), axis=0, keepdims=True)
            total[:, columns] = total[:, columns] * jnp.exp(old_top - new_top) + summed
            top[:, columns] = new_top
        return unused

    lax.fori_loop(0, 7, first_pass, 0)
    top[...] = top[...] + jnp.log(total[...])
    for d in (2, 1, 3):
        out_share(d).wait_recv()
    end_share(1)
    end_share(2)
    gown_ref[...] = gb_ref[:, own_columns]
    upstream = transpose_dot(gb_ref[...], wob_ref[...].reshape(width, gb_ref.shape[1])).astype(BF16).astype(F32)
    spread(upstream, gt, gs)
    products = (upstream * ab_ref[:, own_columns].astype(F32)).T
    for head in range(2):
        rows = products[head * (width // 2) : (head + 1) * (width // 2)]
        delta_ref[:, head * tokens : (head + 1) * tokens] = jnp.sum(rows, axis=0, keepdims=True)

    at[...] = ab_ref[...].astype(F32).T.astype(BF16)
    begin_term(3, dot(at[...], gown_ref[...]))

    def second_pass(turn, unused):
        last = lax.div(turn, 6)
        group = lax.div(turn, 2)
        slot = (1 + 2 * lax.rem(group + 2, 3) + lax.rem(turn, 2)) * (1 - last)

        @pl.when(turn < 6)
        def _():
            arrived(1, slot).wait_recv()

        kt[...] = kv[slot, 0].astype(F32).T.astype(BF16)
        for c in range(4):
            columns = slice(c * chunk, (c + 1) * chunk)
            p = jnp.exp(scores[slot, :, columns] - top[:, columns]).astype(BF16)
            prob[:, columns] = p
            dp = dot(kv[slot, 1], gt[:, columns])
            ds = (p.astype(F32) * (dp - delta_ref[:, columns])).astype(BF16)
            grad[:, columns] = ds
            dqt[:, columns] += dot(kt[...], ds)
        part[slot, 0] = dot(grad[...], qs[...]).astype(BF16)
        part[slot, 1] = dot(prob[...], gs[...]).astype(BF16)

        @pl.when(turn < 6)
        def _():
            homeward(slot).start()

        return unused

    lax.fori_loop(0, 7, second_pass, 0)
    middle = width // 2
    turned = jnp.concatenate([dqt[:middle, :tokens], dqt[middle:, tokens:]], axis=0) * 0.125
    dq = turned.T.astype(BF16)
    begin_term(0, dot(ft[...], dq))
    across = transpose_dot(dq, w3_ref[0].reshape(tokens, width))
    for i in range(3):
        to_y[i].wait_send()
        to_z[i].wait_send()
        onward[i].wait_send()
        for d in order:
            weight_copy(i, d).wait_send()
        for d in (2, 1, 3):
            weight_share(i, d).wait_send()
    for d in (2, 1, 3):
        out_share(d).wait_send()
    for zh in range(4):

        @pl.when(jnp.logical_and(out_from, 2 * zh + out_core != gz))
        def _():
            out_copy(zh).wait_send()

    for i in range(2):
        for k in range(6):
            outward(i, k).wait_send()
    for slot in (5, 6, 1, 2, 3, 4):
        homeward(slot).wait()
    for i in range(2):
        whole = part[0, i].astype(F32)
        for slot in range(1, 7):
            whole = whole + back[slot, i].astype(F32)
        pair_grad = whole.astype(BF16)
        begin_term(1 + i, dot(ft[...], pair_grad))
        across = across + transpose_dot(pair_grad, w3_ref[1 + i].reshape(tokens, width))
    partial_x[...] = across.astype(BF16)

    def join(copies):
        for copy in copies:
            copy.wait()

    def run(copies):
        for copy in copies:
            copy.start()

    owners = (
        (2 * (1 - y_bit) + 1 - z_bit, pair_both),
        (2 * (1 - y_bit) + z_bit, pair_y),
        (2 * y_bit + 1 - z_bit, pair_z),
    )
    g_copies = [
        remote(partial_x.at[slot_rows(slot)], gr.at[k], gsend.at[k], grecv.at[k], device)
        for k, (slot, device) in enumerate(owners)
    ]
    run(g_copies)
    for m in (3, 0, 1, 2):
        for d in (2, 1, 3):
            reduce_x(m, d).wait()
    whole = terms[x].astype(F32)
    for d in range(3):
        whole = whole + xr[d].astype(F32)
    s1[...] = whole.astype(BF16)
    y_copies = []
    for d in (4, 3, 5, 2, 6, 1, 7):
        target = lax.rem(gx + d, 8)
        y_copies.append(remote(s1.at[target], yr.at[d - 1], ysend.at[d - 1], yrecv.at[d - 1], {"gx": target}))
    run(y_copies)
    join(y_copies)
    whole = s1[gx].astype(F32)
    for d in range(7):
        whole = whole + yr[d].astype(F32)
    s2[...] = whole.reshape(8, 8, 128)
    z_copies = []
    for d in (4, 3, 5, 2, 6, 1, 7):
        target = lax.rem(gz + d, 8)
        z_copies.append(remote(s2.at[target], zr.at[gz], zsend.at[d - 1], zrecv.at[d - 1], {"gz": target}))
    run(z_copies)
    zr[gz] = s2[gz]
    join(z_copies)
    lower = zr[0] + zr[2] + zr[4] + zr[6]
    upper = zr[1] + zr[3] + zr[5] + zr[7]
    u[gx] = jnp.concatenate([lower, upper], axis=0).astype(BF16)
    u_copies = []
    for d in (4, 3, 5, 2, 6, 1, 7):
        u_copies.append(remote(u.at[gx], u.at[gx], usend.at[d - 1], urecv.at[d - 1], ring("gx", gx, d)))
    run(u_copies)
    join(g_copies)
    whole = partial_x[mine].astype(F32)
    for k in range(3):
        whole = whole + gr[k].astype(F32)
    gx_ref[...] = whole.astype(BF16)
    join(u_copies)
    h_copies = []
    for d in (4, 3, 5, 2, 6, 1, 7):
        h_copies.append(remote(u, h_ref.at[gy], hsend.at[d - 1], hrecv.at[d - 1], ring("gy", gy, d)))
    run(h_copies)
    h_ref[gy] = u[...]
    join(h_copies)


def finish_kernel(h_ref, g_ref, gx_ref, *out_refs):
    for gy in range(8):
        for gx in range(8):
            x, y_bit, m, r = gy // 2, gy % 2, gx // 2, gx % 2
            tile = h_ref[gy, gx].astype(F32)
            for z_bit in range(2):
                column = (2 * z_bit + y_bit) * 128
                out_refs[m][16 * x + 8 * r : 16 * x + 8 * r + 8, column : column + 128] = tile[8 * z_bit : 8 * z_bit + 8]
    for i in range(gx_ref.shape[0]):
        rows = g_ref[16 * i : 16 * i + 16].astype(F32)
        for j in range(4):
            gx_ref[i, j] = rows[4 * j : 4 * j + 4].astype(BF16)


def vmem(count):
    return [pl.BlockSpec(memory_space=pltpu.VMEM)] * count


def dma(*shape):
    return pltpu.SemaphoreType.DMA(shape)


def call(kernel, number, shapes, scratch, *operands):
    return pl.pallas_call(
        kernel,
        out_shape=[jax.ShapeDtypeStruct(shape, BF16) for shape in shapes],
        in_specs=vmem(len(operands)),
        out_specs=vmem(len(shapes)),
        scratch_shapes=scratch,
        compiler_params=pltpu.CompilerParams(collective_id=number, has_side_effects=True),
    )(*operands)


def transpose_dot(left, right):
    return lax.dot_general(left, right, (((1,), (1,)), ((), ())), preferred_element_type=F32)


def dot(left, right):
    return jnp.dot(left, right, preferred_element_type=F32)


def on_device(features, grad_y, attn_out, w_query, w_key, w_value, w_out):
    width = features.shape[3]
    local = features.shape[0] * features.shape[1] * features.shape[2]
    tokens = 4 * local
    quarter = width // 4
    rows, grad_x = call(
        block_kernel,
        0,
        [(8, 8, 16, quarter), (local, width)],
        [
            pltpu.VMEM((local, width), BF16),
            pltpu.VMEM((local, width), BF16),
            pltpu.VMEM((local, width), BF16),
            pltpu.VMEM((local, width), F32),
            pltpu.VMEM((tokens, width), BF16),
            pltpu.VMEM((tokens, width), BF16),
            pltpu.VMEM((tokens, quarter), BF16),
            pltpu.VMEM((3, 8, 4, 16, quarter), BF16),
            pltpu.VMEM((width, tokens), BF16),
            pltpu.VMEM((width, tokens), BF16),
            pltpu.VMEM((tokens, width), BF16),
            pltpu.VMEM((2, 4, 16, width), BF16),
            pltpu.VMEM((2, tokens, quarter), BF16),
            pltpu.VMEM((1, 2 * tokens), F32),
            pltpu.VMEM((7, 2, tokens, quarter), BF16),
            pltpu.VMEM((7, tokens, 2 * tokens), F32),
            pltpu.VMEM((7, 2, tokens, quarter), BF16),
            pltpu.VMEM((7, 2, tokens, quarter), BF16),
            pltpu.VMEM((quarter, 2 * tokens), BF16),
            pltpu.VMEM((quarter, 2 * tokens), BF16),
            pltpu.VMEM((quarter, tokens), BF16),
            pltpu.VMEM((2 * tokens, quarter), BF16),
            pltpu.VMEM((2 * tokens, quarter), BF16),
            pltpu.VMEM((tokens, 2 * tokens), BF16),
            pltpu.VMEM((tokens, 2 * tokens), BF16),
            pltpu.VMEM((quarter, 2 * tokens), F32),
            pltpu.VMEM((1, 2 * tokens), F32),
            pltpu.VMEM((1, 2 * tokens), F32),
            pltpu.VMEM((4, 8, 64, quarter), BF16),
            pltpu.VMEM((tokens, width), BF16),
            pltpu.VMEM((3, 8, 64, quarter), BF16),
            pltpu.VMEM((8, 64, quarter), BF16),
            pltpu.VMEM((7, 64, quarter), BF16),
            pltpu.VMEM((8, 8, quarter), F32),
            pltpu.VMEM((8, 8, quarter), F32),
            pltpu.VMEM((8, 16, quarter), BF16),
            pltpu.VMEM((3, local, width), BF16),
            dma(3, 3), dma(3, 3), dma(7, 3), dma(7, 3), dma(4), dma(2), dma(3, 4), dma(3, 4),
            dma(2, 7), dma(2, 7), dma(7), dma(7),
            dma(3, 4), dma(3, 4), dma(7), dma(7), dma(7), dma(7), dma(7), dma(7), dma(7), dma(7), dma(3), dma(3),
        ],
        features, grad_y, attn_out, w_query, w_key, w_value, w_out,
    )
    outs = pl.pallas_call(
        finish_kernel,
        out_shape=[jax.ShapeDtypeStruct(features.shape, BF16)] + [jax.ShapeDtypeStruct((64, width), F32)] * 4,
        in_specs=vmem(2),
        out_specs=vmem(5),
    )(rows, grad_x)
    return tuple(outs)


def solution(mesh):
    token_spec = P("gx", "gy", "gz", None)
    row_spec = P("gz", None)
    return jax.shard_map(
        on_device,
        mesh=mesh,
        in_specs=(token_spec,) * 3 + (row_spec,) * 4,
        out_specs=(token_spec,) + (row_spec,) * 4,
        check_vma=False,
    )
```
